256 devices in a mesh: east: 32 (over z, y_hi, core), north: 8 (over x, y_lo).
Axes of the slice: x: 4, y: 4 (y_hi: 2, y_lo: 2; y = y_hi * 2 + y_lo), z: 8, core: 2. Of those that a mesh axis runs over, the one named last changes fastest.
Arguments:
- features: bfloat16 [96, 256, 128, 8], P(None, 'east', 'north'), may hold values from -6 to 6
- brick_active: int32 [32, 16, 1], P('east', 'north'), may hold values 0 or 1
- voxel_occupancy: int32 [256, 128, 8], P('east', 'north'), may hold values 0 or 1
- first_weights: bfloat16 [27, 96, 96], replicated, may hold values from -0.125 to 0.125
- second_weights: bfloat16 [27, 96, 96], replicated, may hold values from -0.125 to 0.125
- head: bfloat16 [13, 96], replicated, may hold values from -0.625 to 0.625
- teacher: bfloat16 [13, 256, 128, 8], P(None, 'east', 'north'), may hold values from -6 to 6
Outputs:
- grad_features: bfloat16 [96, 256, 128, 8], P(None, 'east', 'north')
- grad_first: float32 [27, 96, 96], replicated
- grad_second: float32 [27, 96, 96], replicated
The draws below stay inside these ranges and needn't reach their ends.
All inputs are finite; a program needn't handle non-finite values. No bound on the sum of `brick_active` or of `voxel_occupancy` on one device may be relied on, other than what follows from the above.
Results may differ from the reference program's by a relative error of at most 0.0058.
Values may be sent and summed in bfloat16 or wider, within the bound.
A program may use at most 128 MiB of HBM per device.

```python
import jax
import jax.numpy as jnp
from jax import lax

CHANNELS = 96
CLASSES = 13
BRICK = 8
BE = 1
BN = 2
BZ = 1
EAST_V = 256
NORTH_V = 128
UP_V = 8
VOXELS = 262144
N_EAST = 32
N_NORTH = 8


def set_ends(drawn, own_key, smallest, top_value):
    longest = drawn.shape.index(max(drawn.shape))
    spots = []
    for shift in (0, 1):
        where = [jax.random.randint(jax.random.fold_in(own_key, axis), (), 0, length) for axis, length in enumerate(drawn.shape)]
        where[longest] = (where[longest] + shift) % drawn.shape[longest]
        spots.append(tuple(where))
    return drawn.at[spots[0]].set(smallest).at[spots[1]].set(top_value)


def level_of(stream_key, dims, shards, least, top_value):
    def one(position, blocks):
        draws = jax.random.uniform(jax.random.fold_in(jax.random.fold_in(stream_key, 6), position), (blocks,), jnp.float32, least / len(shards), top_value / len(shards))
        return jnp.repeat(jnp.exp(draws), dims[position] // blocks).reshape((-1,) + (1,) * (len(dims) - position - 1))

    loudness = one(*shards[0])
    for cut in shards[1:]:
        loudness = loudness * one(*cut)
    return loudness


def gaussian(stream_key, shape, spread, bound, cuts=(), held_as=jnp.bfloat16):
    result = jax.random.normal(stream_key, shape, jnp.float32) * spread
    if len(cuts) > 0:
        result = level_of(stream_key, shape, cuts, -0.22, 0.18) * result
    return jnp.clip(result, min=-bound, max=bound).astype(held_as)


def setup_inputs(seed: int = 0) -> dict:
    splits = jax.random.split(jax.random.key(seed), 8)
    features = gaussian(splits[0], (CHANNELS, EAST_V, NORTH_V, UP_V), 1.0, 6.0, ((1, 32), (2, 8)))
    brick_active = set_ends((jax.random.randint(splits[1], (BE * N_EAST, BN * N_NORTH, BZ), 0, 3) < 2).astype(jnp.int32), jax.random.fold_in(splits[1], 1), 0, 1)
    voxel_occupancy = set_ends((jax.random.randint(splits[2], (EAST_V, NORTH_V, UP_V), 0, 2) < 1).astype(jnp.int32), jax.random.fold_in(splits[2], 1), 0, 1)
    first_weights = gaussian(splits[3], (27, CHANNELS, CHANNELS), (27 * CHANNELS) ** -0.5, 0.125)
    second_weights = gaussian(splits[4], (27, CHANNELS, CHANNELS), (27 * CHANNELS) ** -0.5, 0.125)
    head = gaussian(splits[5], (CLASSES, CHANNELS), CHANNELS ** -0.5, 0.625)
    teacher = gaussian(splits[6], (CLASSES, EAST_V, NORTH_V, UP_V), 1.0, 6.0, ((1, 32), (2, 8)))
    return dict(features=features, brick_active=brick_active, voxel_occupancy=voxel_occupancy, first_weights=first_weights, second_weights=second_weights, head=head, teacher=teacher)


def offset_of(k):
    return (k // 9 - 1, k // 3 % 3 - 1, k % 3 - 1)

def shifted(padded, k, sign, shape):
    de, dn, du = offset_of(k)
    east, north, upward = shape
    a = 1 + sign * de
    b = 1 + sign * dn
    c = 1 + sign * du
    piece = padded[:, a:a + east, b:b + north, c:c + upward]
    return piece.reshape(padded.shape[0], -1)

def bordered(field):
    return jnp.pad(field, ((0, 0), (1, 1), (1, 1), (1, 1)))

def silu_slope(value):
    sig = jax.nn.sigmoid(value)
    return sig * (1.0 + value * (1.0 - sig))

def apply_stencil(field, weights, sign):
    shape = field.shape[1:]
    padded = bordered(field)
    total = jnp.zeros((weights.shape[1], field.shape[1] * field.shape[2] * field.shape[3]), jnp.float32)
    for k in range(27):
        piece = shifted(padded, k, sign, shape)
        if sign > 0:
            total = total + jnp.dot(weights[k], piece, preferred_element_type=jnp.float32)
        else:
            total = total + jnp.dot(weights[k].T, piece, preferred_element_type=jnp.float32)
    return total.reshape((weights.shape[1],) + shape)

def kernel_grad(grad, field):
    shape = field.shape[1:]
    padded = bordered(field)
    flat = grad.reshape(grad.shape[0], -1)
    rows = []
    for k in range(27):
        piece = shifted(padded, k, 1, shape)
        rows.append(jnp.dot(flat, piece.T, preferred_element_type=jnp.float32))
    return jnp.stack(rows, 0)

def reference(features, brick_active, voxel_occupancy, first_weights, second_weights, head, teacher):
    flags = jnp.repeat(jnp.repeat(jnp.repeat(brick_active, BRICK, 0), BRICK, 1), BRICK, 2)
    mask = (flags * voxel_occupancy).astype(jnp.float32)
    a0 = jnp.where(mask > 0, features, jnp.zeros_like(features))
    p1 = mask * apply_stencil(a0, first_weights, 1)
    a1 = jax.nn.silu(p1).astype(jnp.bfloat16)
    p2 = mask * apply_stencil(a1, second_weights, 1)
    a2 = jax.nn.silu(p2).astype(jnp.bfloat16)
    channels = a2.shape[0]
    flat_mask = mask.reshape(1, -1)
    logits = jnp.dot(head, a2.reshape(channels, -1), preferred_element_type=jnp.float32)
    g_logits = flat_mask * (logits - teacher.reshape(teacher.shape[0], -1).astype(jnp.float32))
    g_a2 = jnp.dot(head.astype(jnp.float32).T, g_logits, precision=lax.Precision.HIGHEST)
    g_p2 = (flat_mask * g_a2 * silu_slope(p2.reshape(channels, -1))).astype(jnp.bfloat16).reshape(p2.shape)
    scale = 1.0 / jnp.sqrt(jnp.float32(VOXELS))
    grad_second = kernel_grad(g_p2, a1) * scale
    g_a1 = apply_stencil(g_p2, second_weights, -1)
    g_p1 = (mask * g_a1 * silu_slope(p1)).astype(jnp.bfloat16)
    grad_first = kernel_grad(g_p1, a0) * scale
    grad_features = (mask * apply_stencil(g_p1, first_weights, -1)).astype(jnp.bfloat16)
    return (grad_features, grad_first, grad_second)
```

```python
import functools
import math

import jax
import jax.numpy as jnp
from jax import lax
from jax.experimental import pallas as pl
from jax.experimental.pallas import tpu as pltpu
from jax.sharding import PartitionSpec as P

MESH = pl.DeviceIdType.MESH
VM = pltpu.VMEM
F32 = jnp.float32
BF = jnp.bfloat16
SIDES = tuple((a, b) for a in (-1, 0, 1) for b in (-1, 0, 1) if (a, b) != (0, 0))
NT = (((1,), (1,)), ((), ()))


def part(side, size):
    if side > 0:
        return size - 2, 2, 0
    if side < 0:
        return 0, 2, size + 2
    return 0, size, 2


def exchange_start(x_ref, ext_ref, send, recv, local):
    east, north = lax.axis_size("east"), lax.axis_size("north")
    e, n = lax.axis_index("east"), lax.axis_index("north")
    size_e, size_n = x_ref.shape[0], x_ref.shape[1] // 8
    barrier = pltpu.get_barrier_semaphore()

    def peer(side):
        return (lax.rem(e + side[0] + east, east), lax.rem(n + side[1] + north, north))

    for side in SIDES:
        pl.semaphore_signal(barrier, inc=1, device_id=peer(side), device_id_type=MESH)
    centre = pltpu.make_async_copy(
        x_ref, ext_ref.at[pl.ds(2, size_e), pl.ds(16, size_n * 8)], local
    )
    centre.start()
    pl.semaphore_wait(barrier, len(SIDES))
    copies = [centre]
    for i, side in enumerate(SIDES):
        se, le, de = part(side[0], size_e)
        sn, ln, dn = part(side[1], size_n)
        copy = pltpu.make_async_remote_copy(
            src_ref=x_ref.at[pl.ds(se, le), pl.ds(sn * 8, ln * 8)],
            dst_ref=ext_ref.at[pl.ds(de, le), pl.ds(dn * 8, ln * 8)],
            send_sem=send.at[i],
            recv_sem=recv.at[i],
            device_id=peer(side),
            device_id_type=MESH,
        )
        copy.start()
        copies.append(copy)
    return copies


def exchange_end(copies, ext_ref):
    for copy in copies:
        copy.wait()
    e, n = lax.axis_index("east"), lax.axis_index("north")
    wide_e, wide_n, lanes = ext_ref.shape

    @pl.when(e == 0)
    def _():
        ext_ref[0:2] = jnp.zeros((2, wide_n, lanes), ext_ref.dtype)

    @pl.when(e == lax.axis_size("east") - 1)
    def _():
        ext_ref[wide_e - 2 : wide_e] = jnp.zeros((2, wide_n, lanes), ext_ref.dtype)

    @pl.when(n == 0)
    def _():
        ext_ref[:, 0:16] = jnp.zeros((wide_e, 16, lanes), ext_ref.dtype)

    @pl.when(n == lax.axis_size("north") - 1)
    def _():
        ext_ref[:, wide_n - 16 : wide_n] = jnp.zeros((wide_e, 16, lanes), ext_ref.dtype)


def build(src_ref, first, planes, start, count, out_ref):
    wide = src_ref.shape[1] // 8
    up = lax.broadcasted_iota(jnp.int32, (wide, 8, 128), 1)

    def body(i, carry):
        x = src_ref[first + i].astype(F32).reshape(wide, 8, 128)
        below = jnp.where(up == 0, 0.0, pltpu.roll(x, 1, 1))
        above = jnp.where(up == 7, 0.0, pltpu.roll(x, 7, 1))
        rows = pl.ds(pl.multiple_of(i * (count * 8), 16), count * 8)
        for dn in range(3):
            for du, piece in enumerate((below, x, above)):
                block = (dn * 3 + du) * 128
                y = piece[start + dn : start + dn + count].reshape(count * 8, 128)
                out_ref[rows, block : block + 128] = y.astype(BF)
        return carry

    lax.fori_loop(0, planes, body, 0)


def lay_forward(w_ref, out_ref):
    out_ref[...] = jnp.zeros_like(out_ref)
    size = w_ref.shape[1]
    for k in range(27):
        out_ref[k // 9, 0:size, (k % 9) * 128 : (k % 9) * 128 + size] = w_ref[k]


def lay_backward(w_ref, out_ref):
    out_ref[...] = jnp.zeros_like(out_ref)
    size = w_ref.shape[1]
    for k in range(27):
        out_ref[k // 9, (k % 9) * 128 : (k % 9) * 128 + size, 0:size] = w_ref[26 - k]


def convolve(x_ref, plane, rows, w_ref, acc_ref, transposed):
    acc_ref[0:rows] = jnp.zeros((rows, 128), F32)

    def body(i, carry):
        x = x_ref[pl.ds(pl.multiple_of(i * plane, 16), rows)]
        if transposed:
            y = lax.dot_general(x, w_ref[i], NT, preferred_element_type=F32)
        else:
            y = jnp.dot(x, w_ref[i], preferred_element_type=F32)
        acc_ref[0:rows] += y
        return carry

    lax.fori_loop(0, 3, body, 0)


def weight_grad(g_ref, x_ref, plane, out_ref):
    size = out_ref.shape[1]

    def body(i, carry):
        x = x_ref[pl.ds(pl.multiple_of(i * plane, 16), g_ref.shape[1])]
        y = jnp.dot(g_ref[...], x, preferred_element_type=F32)
        for b in range(9):
            out_ref[i * 9 + b] = y[0:size, b * 128 : b * 128 + size]
        return carry

    lax.fori_loop(0, 3, body, 0)


def slope_of(value, sig):
    return sig * (1.0 + value * (1.0 - sig))


def forward_kernel(
    x_ref, w1_ref, w2_ref, head_ref, teacher_ref,
    g2_ref, ext_out, slope_out, grad_ref,
    ext_ref, wf1, wf2, cols1, cols2, acc, a1_ref, gt_ref,
    send, recv, local,
):
    copies = exchange_start(x_ref, ext_ref, send, recv, local)
    lay_forward(w1_ref, wf1)
    lay_forward(w2_ref, wf2)
    exchange_end(copies, ext_ref)
    size_e, rows = x_ref.shape[0], x_ref.shape[1]
    north = rows // 8
    wide = rows + 16
    channels = w1_ref.shape[1]
    ext_out[...] = ext_ref[...]
    build(ext_ref, 0, size_e + 4, 0, north + 2, cols1)
    convolve(cols1, wide, (size_e + 2) * wide, wf1, acc, True)

    def first(i, carry):
        at = pl.ds(pl.multiple_of(i * wide, 16), wide)
        x = ext_ref[i + 1].astype(F32)[8 : 8 + wide]
        mask = jnp.broadcast_to(x[:, channels : channels + 1], (wide, 128))
        p1 = mask * acc[at]
        sig = jax.nn.sigmoid(p1)
        a1_ref[i] = (p1 * sig).astype(BF)
        slope_out[at] = mask * slope_of(p1, sig)
        return carry

    lax.fori_loop(0, size_e + 2, first, 0)
    build(a1_ref, 0, size_e + 2, 0, north, cols2)
    convolve(cols2, rows, size_e * rows, wf2, acc, True)
    head = head_ref[...]

    def second(i, carry):
        at = pl.ds(pl.multiple_of(i * rows, 16), rows)
        x = ext_ref[i + 2, 16 : 16 + rows].astype(F32)
        mask = jnp.broadcast_to(x[:, channels : channels + 1], (rows, 128))
        p2 = mask * acc[at]
        sig = jax.nn.sigmoid(p2)
        a2 = (p2 * sig).astype(BF)
        logits = lax.dot_general(a2, head, NT, preferred_element_type=F32)
        g = mask * (logits - teacher_ref[i].astype(F32))
        high = g.astype(BF)
        rest = g - high.astype(F32)
        mid = rest.astype(BF)
        low = (rest - mid.astype(F32)).astype(BF)
        back = jnp.dot(low, head, preferred_element_type=F32)
        back = back + jnp.dot(mid, head, preferred_element_type=F32)
        back = back + jnp.dot(high, head, preferred_element_type=F32)
        g2 = (mask * back * slope_of(p2, sig)).astype(BF)
        g2_ref[i] = g2
        gt_ref[:, at] = g2.astype(F32).T.astype(BF)
        return carry

    lax.fori_loop(0, size_e, second, 0)
    weight_grad(gt_ref, cols2, rows, grad_ref)


def backward_kernel(
    g2_ref, w1_ref, w2_ref, ext0_ref, slope_ref,
    out_ref, grad_ref,
    ext_ref, wb1, wb2, cols0, cols1, cols2, acc, g1_ref, gt_ref,
    send, recv, local,
):
    copies = exchange_start(g2_ref, ext_ref, send, recv, local)
    size_e, rows = g2_ref.shape[0], g2_ref.shape[1]
    north = rows // 8
    wide = rows + 16
    channels = w1_ref.shape[1]
    lay_backward(w1_ref, wb1)
    lay_backward(w2_ref, wb2)
    build(ext0_ref, 1, size_e + 2, 1, north, cols0)
    exchange_end(copies, ext_ref)
    build(ext_ref, 0, size_e + 4, 0, north + 2, cols1)
    convolve(cols1, wide, (size_e + 2) * wide, wb2, acc, False)

    def first(i, carry):
        at = pl.ds(pl.multiple_of(i * wide, 16), wide)
        g1_ref[i] = (acc[at] * slope_ref[at]).astype(BF)
        return carry

    lax.fori_loop(0, size_e + 2, first, 0)

    def turn(i, carry):
        at = pl.ds(pl.multiple_of(i * rows, 16), rows)
        gt_ref[:, at] = g1_ref[i + 1].astype(F32)[8 : 8 + rows].T.astype(BF)
        return carry

    lax.fori_loop(0, size_e, turn, 0)
    weight_grad(gt_ref, cols0, rows, grad_ref)
    build(g1_ref, 0, size_e + 2, 0, north, cols2)
    convolve(cols2, rows, size_e * rows, wb1, acc, False)

    def last(i, carry):
        at = pl.ds(pl.multiple_of(i * rows, 16), rows)
        x = ext0_ref[i + 2, 16 : 16 + rows].astype(F32)
        mask = jnp.broadcast_to(x[:, channels : channels + 1], (rows, 128))
        out_ref[i] = (mask * acc[at])[:, 0:channels].astype(BF)
        return carry

    lax.fori_loop(0, size_e, last, 0)


def call(kernel, ident, outs, scratch, *args):
    return pl.pallas_call(
        kernel,
        out_shape=outs,
        in_specs=[pl.BlockSpec(memory_space=VM)] * len(args),
        out_specs=[pl.BlockSpec(memory_space=VM)] * len(outs),
        scratch_shapes=scratch,
        compiler_params=pltpu.CompilerParams(
            collective_id=ident, has_side_effects=True, vmem_limit_bytes=60 << 20
        ),
    )(*args)


def per_device(
    features, brick_active, voxel_occupancy, first_weights, second_weights, head, teacher
):
    channels, east, north, upward = features.shape
    classes = head.shape[0]
    rows = north * upward
    flags = jnp.repeat(brick_active, east // brick_active.shape[0], 0)
    flags = jnp.repeat(flags, north // brick_active.shape[1], 1)
    flags = jnp.repeat(flags, upward // brick_active.shape[2], 2)
    mask = (flags * voxel_occupancy)[..., None]
    a0 = features.transpose(1, 2, 3, 0)
    a0 = jnp.where(mask > 0, a0, jnp.zeros_like(a0))
    a0 = jnp.pad(a0, ((0, 0), (0, 0), (0, 0), (0, 128 - channels)))
    lane = lax.broadcasted_iota(jnp.int32, (1, 1, 1, 128), 3)
    x0 = jnp.where(lane == channels, mask.astype(BF), a0).reshape(east, rows, 128)
    wide_teacher = jnp.pad(teacher.transpose(1, 2, 3, 0), ((0, 0), (0, 0), (0, 0), (0, 128 - classes)))
    wide_teacher = wide_teacher.reshape(east, rows, 128)
    wide_head = jnp.pad(head, ((0, 128 - classes), (0, 128 - channels)))
    shape = jax.ShapeDtypeStruct
    sems = [pltpu.SemaphoreType.DMA((8,)), pltpu.SemaphoreType.DMA((8,)), pltpu.SemaphoreType.DMA]
    big = (east + 2) * (rows + 16)
    ext = (east + 4, rows + 32, 128)
    grad = shape((27, channels, channels), F32)
    g2, ext0, slope, second_part = call(
        forward_kernel,
        1,
        (shape((east, rows, 128), BF), shape(ext, BF), shape((big, 128), F32), grad),
        [
            VM(ext, BF),
            VM((3, 128, 1152), BF),
            VM((3, 128, 1152), BF),
            VM(((east + 4) * (rows + 16), 1152), BF),
            VM(((east + 2) * rows, 1152), BF),
            VM((big, 128), F32),
            VM((east + 2, rows + 16, 128), BF),
            VM((128, east * rows), BF),
        ]
        + sems,
        x0,
        first_weights,
        second_weights,
        wide_head,
        wide_teacher,
    )
    out, first_part = call(
        backward_kernel,
        2,
        (shape((east, rows, channels), BF), grad),
        [
            VM(ext, BF),
            VM((3, 1152, 128), BF),
            VM((3, 1152, 128), BF),
            VM(((east + 2) * rows, 1152), BF),
            VM(((east + 4) * (rows + 16), 1152), BF),
            VM(((east + 2) * rows, 1152), BF),
            VM((big, 128), F32),
            VM((east + 2, rows + 16, 128), BF),
            VM((128, east * rows), BF),
        ]
        + sems,
        g2,
        first_weights,
        second_weights,
        ext0,
        slope,
    )
    grad_features = out.reshape(east, north, upward, channels).transpose(3, 0, 1, 2)
    total_voxels = lax.axis_size("east") * lax.axis_size("north") * east * north * upward
    scale = 1.0 / math.sqrt(total_voxels)
    first_part, second_part = lax.psum((first_part, second_part), ("east", "north"))
    return (grad_features, first_part * scale, second_part * scale)


def solution(mesh):
    in_specs = (
        P(None, "east", "north", None),
        P("east", "north", None),
        P("east", "north", None),
        P(),
        P(),
        P(),
        P(None, "east", "north", None),
    )
    out_specs = (P(None, "east", "north", None), P(), P())
    return jax.shard_map(
        per_device, mesh=mesh, in_specs=in_specs, out_specs=out_specs, check_vma=False
    )
```

```python
import functools
import math

import jax
import jax.numpy as jnp
from jax import lax
from jax.experimental import pallas as pl
from jax.experimental.pallas import tpu as pltpu
from jax.sharding import PartitionSpec as P

MESH = pl.DeviceIdType.MESH
VM = pltpu.VMEM
F32 = jnp.float32
BF = jnp.bfloat16
SIDES = tuple((a, b) for a in (-1, 0, 1) for b in (-1, 0, 1) if (a, b) != (0, 0))
NT = (((1,), (1,)), ((), ()))


def part(side, size):
    if side > 0:
        return size - 2, 2, 0
    if side < 0:
        return 0, 2, size + 2
    return 0, size, 2


def exchange_start(x_ref, ext_ref, send, recv, local, others=()):
    east, north = lax.axis_size("east"), lax.axis_size("north")
    e, n = lax.axis_index("east"), lax.axis_index("north")
    size_e, size_n = x_ref.shape[0], x_ref.shape[1] // 8
    barrier = pltpu.get_barrier_semaphore()

    def peer(side):
        return (lax.rem(e + side[0] + east, east), lax.rem(n + side[1] + north, north))

    for device in [peer(side) for side in SIDES] + list(others):
        pl.semaphore_signal(barrier, inc=1, device_id=device, device_id_type=MESH)
    centre = pltpu.make_async_copy(
        x_ref, ext_ref.at[pl.ds(2, size_e), pl.ds(16, size_n * 8)], local
    )
    centre.start()
    pl.semaphore_wait(barrier, len(SIDES) + len(others))
    copies = [centre]
    for i, side in enumerate(SIDES):
        se, le, de = part(side[0], size_e)
        sn, ln, dn = part(side[1], size_n)
        copy = pltpu.make_async_remote_copy(
            src_ref=x_ref.at[pl.ds(se, le), pl.ds(sn * 8, ln * 8)],
            dst_ref=ext_ref.at[pl.ds(de, le), pl.ds(dn * 8, ln * 8)],
            send_sem=send.at[i],
            recv_sem=recv.at[i],
            device_id=peer(side),
            device_id_type=MESH,
        )
        copy.start()
        copies.append(copy)
    return copies


def exchange_end(copies, ext_ref):
    for copy in copies:
        copy.wait()
    e, n = lax.axis_index("east"), lax.axis_index("north")
    wide_e, wide_n, lanes = ext_ref.shape

    @pl.when(e == 0)
    def _():
        ext_ref[0:2] = jnp.zeros((2, wide_n, lanes), ext_ref.dtype)

    @pl.when(e == lax.axis_size("east") - 1)
    def _():
        ext_ref[wide_e - 2 : wide_e] = jnp.zeros((2, wide_n, lanes), ext_ref.dtype)

    @pl.when(n == 0)
    def _():
        ext_ref[:, 0:16] = jnp.zeros((wide_e, 16, lanes), ext_ref.dtype)

    @pl.when(n == lax.axis_size("north") - 1)
    def _():
        ext_ref[:, wide_n - 16 : wide_n] = jnp.zeros((wide_e, 16, lanes), ext_ref.dtype)


def build(src_ref, first, planes, start, count, out_ref):
    wide = src_ref.shape[1] // 8
    up = lax.broadcasted_iota(jnp.int32, (wide, 8, 128), 1)

    def body(i, carry):
        x = src_ref[first + i].astype(F32).reshape(wide, 8, 128)
        below = jnp.where(up == 0, 0.0, pltpu.roll(x, 1, 1))
        above = jnp.where(up == 7, 0.0, pltpu.roll(x, 7, 1))
        rows = pl.ds(pl.multiple_of(i * (count * 8), 16), count * 8)
        for dn in range(3):
            for du, piece in enumerate((below, x, above)):
                block = (dn * 3 + du) * 128
                y = piece[start + dn : start + dn + count].reshape(count * 8, 128)
                out_ref[rows, block : block + 128] = y.astype(BF)
        return carry

    lax.fori_loop(0, planes, body, 0)


def lay_forward(w_ref, out_ref):
    out_ref[...] = jnp.zeros_like(out_ref)
    size = w_ref.shape[1]
    for k in range(27):
        out_ref[k // 9, 0:size, (k % 9) * 128 : (k % 9) * 128 + size] = w_ref[k]


def lay_backward(w_ref, out_ref):
    out_ref[...] = jnp.zeros_like(out_ref)
    size = w_ref.shape[1]
    for k in range(27):
        out_ref[k // 9, (k % 9) * 128 : (k % 9) * 128 + size, 0:size] = w_ref[26 - k]


def convolve(x_ref, plane, rows, w_ref, acc_ref, transposed):
    acc_ref[0:rows] = jnp.zeros((rows, 128), F32)

    def body(i, carry):
        x = x_ref[pl.ds(pl.multiple_of(i * plane, 16), rows)]
        if transposed:
            y = lax.dot_general(x, w_ref[i], NT, preferred_element_type=F32)
        else:
            y = jnp.dot(x, w_ref[i], preferred_element_type=F32)
        acc_ref[0:rows] += y
        return carry

    lax.fori_loop(0, 3, body, 0)


def weight_grad(g_ref, x_ref, plane, out_ref):
    size = out_ref.shape[1]

    def body(i, carry):
        x = x_ref[pl.ds(pl.multiple_of(i * plane, 16), g_ref.shape[1])]
        y = jnp.dot(g_ref[...], x, preferred_element_type=F32)
        for b in range(9):
            out_ref[i * 9 + b] = y[0:size, b * 128 : (b + 1) * 128]
        return carry

    lax.fori_loop(0, 3, body, 0)


class Place:
    def __init__(self):
        e, n = lax.axis_index("east"), lax.axis_index("north")
        self.core = lax.rem(e, 2)
        self.z = lax.div(e, 4)
        self.zs = lax.axis_size("east") // 4
        self.xs = lax.axis_size("north") // 2
        self.x = lax.div(n, 2)
        self.y = lax.rem(lax.div(e, 2), 2) * 2 + lax.rem(n, 2)

    def device(self, core=None, x=None, y=None, z=None):
        core = self.core if core is None else core
        x = self.x if x is None else x
        y = self.y if y is None else y
        z = self.z if z is None else z
        return (z * 4 + lax.div(y, 2) * 2 + core, x * 2 + lax.rem(y, 2))

    def partner(self):
        return self.device(core=1 - self.core)

    def along(self, axis, step):
        if axis == "x":
            at = lax.rem(self.x + step, self.xs)
            return at, self.device(x=at)
        if axis == "y":
            at = lax.rem(self.y + step, 4)
            return at, self.device(y=at)
        at = lax.rem(self.z + step, self.zs)
        return at, self.device(z=at)

    def peers(self):
        found = [self.partner()]
        for axis, count in (("x", self.xs), ("y", 4), ("z", self.zs)):
            found += [self.along(axis, step)[1] for step in range(1, count)]
        return found


def all_reduce(place, src, full, got_core, held, got_one, one, held_one, got_two, slots, send, recv):
    rows = src.shape[0]
    half = rows // 2
    stream = half // 2
    wide = stream // 4
    piece = wide // 4
    orders = (("x", "y"), ("y", "x"))
    here = {"x": place.x, "y": place.y}
    started = []

    def go(a, b, device):
        i = len(started)
        copy = pltpu.make_async_remote_copy(
            src_ref=a, dst_ref=b, send_sem=send.at[i], recv_sem=recv.at[i],
            device_id=device, device_id_type=MESH,
        )
        copy.start()
        started.append(copy)
        return copy

    def at(start, size):
        return pl.ds(pl.multiple_of(start, 32), size)

    mine = place.core * half
    copies = [go(src.at[at((1 - place.core) * half, half)], got_core, place.partner())]
    yield

    copies.pop().wait_recv()

    def pair(i, carry):
        total = src[at(mine + i * 128, 128)] + got_core[at(i * 128, 128)]
        held[at(i * 128, 128)] = total.astype(BF)
        return carry

    lax.fori_loop(0, half // 128, pair, 0)
    for s, (axis, _) in enumerate(orders):
        for step in range(1, 4):
            there, device = place.along(axis, step)
            copies.append(go(held.at[at(s * stream + there * wide, wide)], got_one.at[s, step - 1], device))
    yield

    for copy in copies:
        copy.wait_recv()
    copies = []
    for s, (axis, other) in enumerate(orders):
        start = s * stream + here[axis] * wide
        total = src[at(mine + start, wide)] + got_core[at(start, wide)]
        for step in range(3):
            total = total + got_one[s, step].astype(F32)
        one[s] = total
        held_one[s] = total.astype(BF)
        for step in range(1, 4):
            there, device = place.along(other, step)
            copies.append(go(held_one.at[s, at(there * piece, piece)], got_two.at[s, step - 1], device))
    yield

    for copy in copies:
        copy.wait_recv()
    copies = []
    for s, (_, other) in enumerate(orders):
        total = one[s, at(here[other] * piece, piece)]
        for step in range(3):
            total = total + got_two[s, step].astype(F32)
        slots[place.z, s * piece : (s + 1) * piece] = total.astype(BF)
    for step in range(1, place.zs):
        _, device = place.along("z", step)
        copies.append(go(slots.at[place.z], slots.at[place.z], device))
    yield

    for copy in copies:
        copy.wait_recv()
    copies = []
    total = slots[0].astype(F32)
    for z in range(1, place.zs):
        total = total + slots[z].astype(F32)
    for s, (axis, other) in enumerate(orders):
        rows_here = at(mine + s * stream + here[axis] * wide + here[other] * piece, piece)
        full[rows_here] = total[s * piece : (s + 1) * piece].astype(BF)
        for step in range(1, 4):
            _, device = place.along(other, step)
            copies.append(go(full.at[rows_here], full.at[rows_here], device))
    yield

    for copy in copies:
        copy.wait_recv()
    copies = []
    for s, (axis, _) in enumerate(orders):
        rows_here = at(mine + s * stream + here[axis] * wide, wide)
        for step in range(1, 4):
            _, device = place.along(axis, step)
            copies.append(go(full.at[rows_here], full.at[rows_here], device))
    yield

    for copy in copies:
        copy.wait_recv()
    copies = [go(full.at[at(mine, half)], full.at[at(mine, half)], place.partner())]
    yield

    copies.pop().wait_recv()
    for copy in started:
        copy.wait_send()
    yield


REDUCE_COPIES = 40


def reduce_scratch(rows, zs):
    half = rows // 2
    return [
        VM((rows, 128), BF),
        VM((half, 128), F32),
        VM((half, 128), BF),
        VM((2, 3, half // 8, 128), BF),
        VM((2, half // 8, 128), F32),
        VM((2, half // 8, 128), BF),
        VM((2, 3, half // 32, 128), BF),
        VM((zs, half // 16, 128), BF),
        pltpu.SemaphoreType.DMA((REDUCE_COPIES,)),
        pltpu.SemaphoreType.DMA((REDUCE_COPIES,)),
    ]


PACKED = 2048


def pack(grad_ref, out_ref):
    size = grad_ref.shape[1]
    lane = lax.broadcasted_iota(jnp.int32, (size, 128), 1)

    def body(g, carry):
        spare = grad_ref[g * 4 + 3]
        for j in range(3):
            moved = pltpu.roll(spare, 96 - 32 * j, 1)
            rows = pl.ds(pl.multiple_of((g * 3 + j) * size, 32), size)
            out_ref[rows] = jnp.where(lane < 96, grad_ref[g * 4 + j], moved)
        return carry

    lax.fori_loop(0, 6, body, 0)
    for j in range(3):
        out_ref[(18 + j) * size : (19 + j) * size] = grad_ref[24 + j]
    out_ref[21 * size :] = jnp.zeros((out_ref.shape[0] - 21 * size, 128), F32)


def unpack(full_ref, out_ref, scale):
    size = out_ref.shape[1]
    lane = lax.broadcasted_iota(jnp.int32, (size, 128), 1)

    def take(block):
        rows = pl.ds(pl.multiple_of(block * size, 32), size)
        return full_ref[rows].astype(F32) * scale

    def body(g, carry):
        spare = []
        for j in range(3):
            value = take(g * 3 + j)
            out_ref[g * 4 + j] = value[:, 0:size]
            spare.append(pltpu.roll(value, 32 + 32 * j, 1))
        value = jnp.where(lane < 32, spare[0], jnp.where(lane < 64, spare[1], spare[2]))
        out_ref[g * 4 + 3] = value[:, 0:size]
        return carry

    lax.fori_loop(0, 6, body, 0)
    for j in range(3):
        out_ref[24 + j] = take(18 + j)[:, 0:size]


def slope_of(value, sig):
    return sig * (1.0 + value * (1.0 - sig))


def forward_kernel(
    x_ref, w1_ref, w2_ref, head_ref, teacher_ref,
    g2_ref, ext_out, slope_out, grad_ref,
    ext_ref, wf1, wf2, cols1, cols2, acc, a1_ref, gt_ref, part_ref,
    send, recv, local,
):
    copies = exchange_start(x_ref, ext_ref, send, recv, local)
    lay_forward(w1_ref, wf1)
    lay_forward(w2_ref, wf2)
    exchange_end(copies, ext_ref)
    size_e, rows = x_ref.shape[0], x_ref.shape[1]
    north = rows // 8
    wide = rows + 16
    channels = w1_ref.shape[1]
    ext_out[...] = ext_ref[...]
    build(ext_ref, 0, size_e + 4, 0, north + 2, cols1)
    convolve(cols1, wide, (size_e + 2) * wide, wf1, acc, True)

    def first(i, carry):
        at = pl.ds(pl.multiple_of(i * wide, 16), wide)
        x = ext_ref[i + 1].astype(F32)[8 : 8 + wide]
        mask = jnp.broadcast_to(x[:, channels : channels + 1], (wide, 128))
        p1 = mask * acc[at]
        sig = jax.nn.sigmoid(p1)
        a1_ref[i] = (p1 * sig).astype(BF)
        slope_out[at] = mask * slope_of(p1, sig)
        return carry

    lax.fori_loop(0, size_e + 2, first, 0)
    build(a1_ref, 0, size_e + 2, 0, north, cols2)
    convolve(cols2, rows, size_e * rows, wf2, acc, True)
    head = head_ref[...]

    def second(i, carry):
        at = pl.ds(pl.multiple_of(i * rows, 16), rows)
        x = ext_ref[i + 2, 16 : 16 + rows].astype(F32)
        mask = jnp.broadcast_to(x[:, channels : channels + 1], (rows, 128))
        p2 = mask * acc[at]
        sig = jax.nn.sigmoid(p2)
        a2 = (p2 * sig).astype(BF)
        logits = lax.dot_general(a2, head, NT, preferred_element_type=F32)
        g = mask * (logits - teacher_ref[i].astype(F32))
        high = g.astype(BF)
        rest = g - high.astype(F32)
        mid = rest.astype(BF)
        low = (rest - mid.astype(F32)).astype(BF)
        back = jnp.dot(low, head, preferred_element_type=F32)
        back = back + jnp.dot(mid, head, preferred_element_type=F32)
        back = back + jnp.dot(high, head, preferred_element_type=F32)
        g2 = (mask * back * slope_of(p2, sig)).astype(BF)
        g2_ref[i] = g2
        gt_ref[:, at] = g2.astype(F32).T.astype(BF)
        return carry

    lax.fori_loop(0, size_e, second, 0)
    weight_grad(gt_ref, cols2, rows, part_ref)
    pack(part_ref, grad_ref)


def backward_kernel(
    scale, g2_ref, w1_ref, w2_ref, ext0_ref, slope_ref, packed2_ref,
    out_ref, grad1_ref, grad2_ref,
    ext_ref, wb1, wb2, cols0, cols1, cols2, acc, g1_ref, gt_ref, part_ref, packed1_ref,
    send, recv, local, *rest,
):
    place = Place()
    half = len(rest) // 2
    copies = exchange_start(g2_ref, ext_ref, send, recv, local, place.peers())
    two = all_reduce(place, packed2_ref, *rest[:half])
    one = all_reduce(place, packed1_ref, *rest[half:])
    next(two)
    size_e, rows = g2_ref.shape[0], g2_ref.shape[1]
    north = rows // 8
    wide = rows + 16
    channels = w1_ref.shape[1]
    lay_backward(w1_ref, wb1)
    lay_backward(w2_ref, wb2)
    next(two)
    build(ext0_ref, 1, size_e + 2, 1, north, cols0)
    exchange_end(copies, ext_ref)
    next(two)
    build(ext_ref, 0, size_e + 4, 0, north + 2, cols1)
    convolve(cols1, wide, (size_e + 2) * wide, wb2, acc, False)
    next(two)

    def first(i, carry):
        at = pl.ds(pl.multiple_of(i * wide, 16), wide)
        g1_ref[i] = (acc[at] * slope_ref[at]).astype(BF)
        return carry

    lax.fori_loop(0, size_e + 2, first, 0)

    def turn(i, carry):
        at = pl.ds(pl.multiple_of(i * rows, 16), rows)
        gt_ref[:, at] = g1_ref[i + 1].astype(F32)[8 : 8 + rows].T.astype(BF)
        return carry

    lax.fori_loop(0, size_e, turn, 0)
    weight_grad(gt_ref, cols0, rows, part_ref)
    pack(part_ref, packed1_ref)
    next(one)
    next(two)
    build(g1_ref, 0, size_e + 2, 0, north, cols2)
    next(one)
    next(two)
    convolve(cols2, rows, size_e * rows, wb1, acc, False)
    next(one)
    next(two)

    def last(i, carry):
        at = pl.ds(pl.multiple_of(i * rows, 16), rows)
        x = ext0_ref[i + 2, 16 : 16 + rows].astype(F32)
        mask = jnp.broadcast_to(x[:, channels : channels + 1], (rows, 128))
        out_ref[i] = (mask * acc[at])[:, 0:channels].astype(BF)
        return carry

    lax.fori_loop(0, size_e, last, 0)
    next(one)
    next(two)
    unpack(rest[0], grad2_ref, scale)
    for _ in one:
        pass
    unpack(rest[half], grad1_ref, scale)


def call(kernel, ident, outs, scratch, *args):
    return pl.pallas_call(
        kernel,
        out_shape=outs,
        in_specs=[pl.BlockSpec(memory_space=VM)] * len(args),
        out_specs=[pl.BlockSpec(memory_space=VM)] * len(outs),
        scratch_shapes=scratch,
        compiler_params=pltpu.CompilerParams(
            collective_id=ident, has_side_effects=True, vmem_limit_bytes=60 << 20
        ),
    )(*args)


def per_device(
    features, brick_active, voxel_occupancy, first_weights, second_weights, head, teacher
):
    channels, east, north, upward = features.shape
    classes = head.shape[0]
    rows = north * upward
    flags = jnp.repeat(brick_active, east // brick_active.shape[0], 0)
    flags = jnp.repeat(flags, north // brick_active.shape[1], 1)
    flags = jnp.repeat(flags, upward // brick_active.shape[2], 2)
    mask = (flags * voxel_occupancy)[..., None]
    a0 = features.transpose(1, 2, 3, 0)
    a0 = jnp.where(mask > 0, a0, jnp.zeros_like(a0))
    a0 = jnp.pad(a0, ((0, 0), (0, 0), (0, 0), (0, 128 - channels)))
    lane = lax.broadcasted_iota(jnp.int32, (1, 1, 1, 128), 3)
    x0 = jnp.where(lane == channels, mask.astype(BF), a0).reshape(east, rows, 128)
    wide_teacher = jnp.pad(teacher.transpose(1, 2, 3, 0), ((0, 0), (0, 0), (0, 0), (0, 128 - classes)))
    wide_teacher = wide_teacher.reshape(east, rows, 128)
    wide_head = jnp.pad(head, ((0, 128 - classes), (0, 128 - channels)))
    shape = jax.ShapeDtypeStruct
    sems = [pltpu.SemaphoreType.DMA((8,)), pltpu.SemaphoreType.DMA((8,)), pltpu.SemaphoreType.DMA]
    big = (east + 2) * (rows + 16)
    ext = (east + 4, rows + 32, 128)
    packed = shape((PACKED, 128), F32)
    part_sums = VM((27, channels, 128), F32)
    grad = shape((27, channels, channels), F32)
    total_voxels = lax.axis_size("east") * lax.axis_size("north") * east * north * upward
    scale = 1.0 / math.sqrt(total_voxels)
    zs = lax.axis_size("east") // 4
    g2, ext0, slope, second_part = call(
        forward_kernel,
        1,
        (shape((east, rows, 128), BF), shape(ext, BF), shape((big, 128), F32), packed),
        [
            VM(ext, BF),
            VM((3, 128, 1152), BF),
            VM((3, 128, 1152), BF),
            VM(((east + 4) * (rows + 16), 1152), BF),
            VM(((east + 2) * rows, 1152), BF),
            VM((big, 128), F32),
            VM((east + 2, rows + 16, 128), BF),
            VM((128, east * rows), BF),
            part_sums,
        ]
        + sems,
        x0,
        first_weights,
        second_weights,
        wide_head,
        wide_teacher,
    )
    out, grad_first, grad_second = call(
        functools.partial(backward_kernel, scale),
        2,
        (shape((east, rows, channels), BF), grad, grad),
        [
            VM(ext, BF),
            VM((3, 1152, 128), BF),
            VM((3, 1152, 128), BF),
            VM(((east + 2) * rows, 1152), BF),
            VM(((east + 4) * (rows + 16), 1152), BF),
            VM(((east + 2) * rows, 1152), BF),
            VM((big, 128), F32),
            VM((east + 2, rows + 16, 128), BF),
            VM((128, east * rows), BF),
            part_sums,
            VM((PACKED, 128), F32),
        ]
        + sems
        + reduce_scratch(PACKED, zs) * 2,
        g2,
        first_weights,
        second_weights,
        ext0,
        slope,
        second_part,
    )
    grad_features = out.reshape(east, north, upward, channels).transpose(3, 0, 1, 2)
    return (grad_features, grad_first, grad_second)


def solution(mesh):
    in_specs = (
        P(None, "east", "north", None),
        P("east", "north", None),
        P("east", "north", None),
        P(),
        P(),
        P(),
        P(None, "east", "north", None),
    )
    out_specs = (P(None, "east", "north", None), P(), P())
    return jax.shard_map(
        per_device, mesh=mesh, in_specs=in_specs, out_specs=out_specs, check_vma=False
    )
```

```python
import functools
import math

import jax
import jax.numpy as jnp
from jax import lax
from jax.experimental import pallas as pl
from jax.experimental.pallas import tpu as pltpu
from jax.sharding import PartitionSpec as P

MESH = pl.DeviceIdType.MESH
VM = pltpu.VMEM
F32 = jnp.float32
BF = jnp.bfloat16
SIDES = tuple((a, b) for a in (-1, 0, 1) for b in (-1, 0, 1) if (a, b) != (0, 0))
NT = (((1,), (1,)), ((), ()))


def part(side, size):
    if side > 0:
        return size - 2, 2, 0
    if side < 0:
        return 0, 2, size + 2
    return 0, size, 2


def around():
    east, north = lax.axis_size("east"), lax.axis_size("north")
    e, n = lax.axis_index("east"), lax.axis_index("north")
    return [(lax.rem(e + a + east, east), lax.rem(n + b + north, north)) for a, b in SIDES]


def exchange_start(ext_ref, send, recv):
    size_e, size_n = ext_ref.shape[0] - 4, ext_ref.shape[1] // 8 - 4
    copies = []
    for i, (side, device) in enumerate(zip(SIDES, around())):
        se, le, de = part(side[0], size_e)
        sn, ln, dn = part(side[1], size_n)
        copy = pltpu.make_async_remote_copy(
            src_ref=ext_ref.at[pl.ds(se + 2, le), pl.ds((sn + 2) * 8, ln * 8)],
            dst_ref=ext_ref.at[pl.ds(de, le), pl.ds(dn * 8, ln * 8)],
            send_sem=send.at[i],
            recv_sem=recv.at[i],
            device_id=device,
            device_id_type=MESH,
        )
        copy.start()
        copies.append(copy)
    return copies


def exchange_end(copies, ext_ref):
    for copy in copies:
        copy.wait()
    e, n = lax.axis_index("east"), lax.axis_index("north")
    wide_e, wide_n, lanes = ext_ref.shape

    @pl.when(e == 0)
    def _():
        ext_ref[0:2] = jnp.zeros((2, wide_n, lanes), ext_ref.dtype)

    @pl.when(e == lax.axis_size("east") - 1)
    def _():
        ext_ref[wide_e - 2 : wide_e] = jnp.zeros((2, wide_n, lanes), ext_ref.dtype)

    @pl.when(n == 0)
    def _():
        ext_ref[:, 0:16] = jnp.zeros((wide_e, 16, lanes), ext_ref.dtype)

    @pl.when(n == lax.axis_size("north") - 1)
    def _():
        ext_ref[:, wide_n - 16 : wide_n] = jnp.zeros((wide_e, 16, lanes), ext_ref.dtype)


def build(src_ref, first, planes, start, count, out_ref):
    wide = src_ref.shape[1] // 8
    up = lax.broadcasted_iota(jnp.int32, (wide, 8, 128), 1)

    def body(i, carry):
        x = src_ref[first + i].astype(F32).reshape(wide, 8, 128)
        below = jnp.where(up == 0, 0.0, pltpu.roll(x, 1, 1))
        above = jnp.where(up == 7, 0.0, pltpu.roll(x, 7, 1))
        rows = pl.ds(pl.multiple_of(i * (count * 8), 16), count * 8)
        for dn in range(3):
            for du, piece in enumerate((below, x, above)):
                block = (dn * 3 + du) * 128
                y = piece[start + dn : start + dn + count].reshape(count * 8, 128)
                out_ref[rows, block : block + 128] = y.astype(BF)
        return carry

    lax.fori_loop(0, planes, body, 0)


def lay_forward(w_ref, out_ref):
    out_ref[...] = jnp.zeros_like(out_ref)
    size = w_ref.shape[1]
    for k in range(27):
        out_ref[k // 9, 0:size, (k % 9) * 128 : (k % 9) * 128 + size] = w_ref[k]


def lay_backward(w_ref, out_ref):
    out_ref[...] = jnp.zeros_like(out_ref)
    size = w_ref.shape[1]
    for k in range(27):
        out_ref[k // 9, (k % 9) * 128 : (k % 9) * 128 + size, 0:size] = w_ref[26 - k]


def convolve(x_ref, plane, rows, w_ref, acc_ref, transposed):
    acc_ref[0:rows] = jnp.zeros((rows, 128), F32)

    def body(i, carry):
        x = x_ref[pl.ds(pl.multiple_of(i * plane, 16), rows)]
        if transposed:
            y = lax.dot_general(x, w_ref[i], NT, preferred_element_type=F32)
        else:
            y = jnp.dot(x, w_ref[i], preferred_element_type=F32)
        acc_ref[0:rows] += y
        return carry

    lax.fori_loop(0, 3, body, 0)


def weight_grad(g_ref, x_ref, plane, out_ref):
    size = out_ref.shape[1]

    def body(i, carry):
        x = x_ref[pl.ds(pl.multiple_of(i * plane, 16), g_ref.shape[1])]
        y = jnp.dot(g_ref[...], x, preferred_element_type=F32)
        for b in range(9):
            out_ref[i * 9 + b] = y[0:size, b * 128 : (b + 1) * 128]
        return carry

    lax.fori_loop(0, 3, body, 0)


class Place:
    def __init__(self):
        e, n = lax.axis_index("east"), lax.axis_index("north")
        self.core = lax.rem(e, 2)
        self.z = lax.div(e, 4)
        self.zs = lax.axis_size("east") // 4
        self.xs = lax.axis_size("north") // 2
        self.x = lax.div(n, 2)
        self.y = lax.rem(lax.div(e, 2), 2) * 2 + lax.rem(n, 2)

    def device(self, core=None, x=None, y=None, z=None):
        core = self.core if core is None else core
        x = self.x if x is None else x
        y = self.y if y is None else y
        z = self.z if z is None else z
        return (z * 4 + lax.div(y, 2) * 2 + core, x * 2 + lax.rem(y, 2))

    def partner(self):
        return self.device(core=1 - self.core)

    def along(self, axis, step):
        if axis == "x":
            at = lax.rem(self.x + step, self.xs)
            return at, self.device(x=at)
        if axis == "y":
            at = lax.rem(self.y + step, 4)
            return at, self.device(y=at)
        at = lax.rem(self.z + step, self.zs)
        return at, self.device(z=at)

    def peers(self):
        found = [self.partner()]
        for axis, count in (("x", self.xs), ("y", 4), ("z", self.zs)):
            found += [self.along(axis, step)[1] for step in range(1, count)]
        return found


def all_reduce(place, src, full, got_core, held, got_one, one, held_one, got_two, slots, send, recv):
    rows = src.shape[0]
    half = rows // 2
    stream = half // 2
    wide = stream // 4
    piece = wide // 4
    orders = (("x", "y"), ("y", "x"))
    here = {"x": place.x, "y": place.y}
    started = []

    def go(a, b, device):
        i = len(started)
        copy = pltpu.make_async_remote_copy(
            src_ref=a, dst_ref=b, send_sem=send.at[i], recv_sem=recv.at[i],
            device_id=device, device_id_type=MESH,
        )
        copy.start()
        started.append(copy)
        return copy

    def at(start, size):
        return pl.ds(pl.multiple_of(start, 32), size)

    mine = place.core * half
    copies = [go(src.at[at((1 - place.core) * half, half)], got_core, place.partner())]
    yield

    copies.pop().wait_recv()

    def pair(i, carry):
        total = src[at(mine + i * 128, 128)] + got_core[at(i * 128, 128)]
        held[at(i * 128, 128)] = total.astype(BF)
        return carry

    lax.fori_loop(0, half // 128, pair, 0)
    for s, (axis, _) in enumerate(orders):
        for step in range(1, 4):
            there, device = place.along(axis, step)
            copies.append(go(held.at[at(s * stream + there * wide, wide)], got_one.at[s, step - 1], device))
    yield

    for copy in copies:
        copy.wait_recv()
    copies = []
    for s, (axis, other) in enumerate(orders):
        start = s * stream + here[axis] * wide
        total = src[at(mine + start, wide)] + got_core[at(start, wide)]
        for step in range(3):
            total = total + got_one[s, step].astype(F32)
        one[s] = total
        held_one[s] = total.astype(BF)
        for step in range(1, 4):
            there, device = place.along(other, step)
            copies.append(go(held_one.at[s, at(there * piece, piece)], got_two.at[s, step - 1], device))
    yield

    for copy in copies:
        copy.wait_recv()
    copies = []
    for s, (_, other) in enumerate(orders):
        total = one[s, at(here[other] * piece, piece)]
        for step in range(3):
            total = total + got_two[s, step].astype(F32)
        slots[place.z, s * piece : (s + 1) * piece] = total.astype(BF)
    for step in range(1, place.zs):
        _, device = place.along("z", step)
        copies.append(go(slots.at[place.z], slots.at[place.z], device))
    yield

    for copy in copies:
        copy.wait_recv()
    copies = []
    total = slots[0].astype(F32)
    for z in range(1, place.zs):
        total = total + slots[z].astype(F32)
    for s, (axis, other) in enumerate(orders):
        rows_here = at(mine + s * stream + here[axis] * wide + here[other] * piece, piece)
        full[rows_here] = total[s * piece : (s + 1) * piece].astype(BF)
        for step in range(1, 4):
            _, device = place.along(other, step)
            copies.append(go(full.at[rows_here], full.at[rows_here], device))
    yield

    for copy in copies:
        copy.wait_recv()
    copies = []
    for s, (axis, _) in enumerate(orders):
        rows_here = at(mine + s * stream + here[axis] * wide, wide)
        for step in range(1, 4):
            _, device = place.along(axis, step)
            copies.append(go(full.at[rows_here], full.at[rows_here], device))
    yield

    for copy in copies:
        copy.wait_recv()
    copies = [go(full.at[at(mine, half)], full.at[at(mine, half)], place.partner())]
    yield

    copies.pop().wait_recv()
    for copy in started:
        copy.wait_send()
    yield


REDUCE_COPIES = 40


def reduce_scratch(rows, zs):
    half = rows // 2
    return [
        VM((rows, 128), BF),
        VM((half, 128), F32),
        VM((half, 128), BF),
        VM((2, 3, half // 8, 128), BF),
        VM((2, half // 8, 128), F32),
        VM((2, half // 8, 128), BF),
        VM((2, 3, half // 32, 128), BF),
        VM((zs, half // 16, 128), BF),
        pltpu.SemaphoreType.DMA((REDUCE_COPIES,)),
        pltpu.SemaphoreType.DMA((REDUCE_COPIES,)),
    ]


PACKED = 2048


def pack(grad_ref, out_ref):
    size = grad_ref.shape[1]
    lane = lax.broadcasted_iota(jnp.int32, (size, 128), 1)

    def body(g, carry):
        spare = grad_ref[g * 4 + 3]
        for j in range(3):
            moved = pltpu.roll(spare, 96 - 32 * j, 1)
            rows = pl.ds(pl.multiple_of((g * 3 + j) * size, 32), size)
            out_ref[rows] = jnp.where(lane < 96, grad_ref[g * 4 + j], moved)
        return carry

    lax.fori_loop(0, 6, body, 0)
    for j in range(3):
        out_ref[(18 + j) * size : (19 + j) * size] = grad_ref[24 + j]
    out_ref[21 * size :] = jnp.zeros((out_ref.shape[0] - 21 * size, 128), F32)


def unpack(full_ref, out_ref, scale):
    size = out_ref.shape[1]
    lane = lax.broadcasted_iota(jnp.int32, (size, 128), 1)

    def take(block):
        rows = pl.ds(pl.multiple_of(block * size, 32), size)
        return full_ref[rows].astype(F32) * scale

    def body(g, carry):
        spare = []
        for j in range(3):
            value = take(g * 3 + j)
            out_ref[g * 4 + j] = value[:, 0:size]
            spare.append(pltpu.roll(value, 32 + 32 * j, 1))
        value = jnp.where(lane < 32, spare[0], jnp.where(lane < 64, spare[1], spare[2]))
        out_ref[g * 4 + 3] = value[:, 0:size]
        return carry

    lax.fori_loop(0, 6, body, 0)
    for j in range(3):
        out_ref[24 + j] = take(18 + j)[:, 0:size]


def slope_of(value, sig):
    return sig * (1.0 + value * (1.0 - sig))


def lay_teacher(teacher_ref, flat_ref, out_ref):
    classes, east, up, north = teacher_ref.shape
    flat_ref[...] = teacher_ref[...].astype(F32).reshape(flat_ref.shape)
    rows = classes * east
    parts = [flat_ref[pl.ds(u, rows, stride=up), :] for u in range(up)]
    wide = jnp.concatenate(parts, axis=1).astype(BF)
    wide = jnp.concatenate([wide, jnp.zeros((128 - rows, 128), BF)], axis=0)
    turned = lax.dot_general(reorder(up, north), wide, NT, preferred_element_type=F32)
    out_ref[...] = turned.astype(BF)


def reorder(up, north):
    row = lax.broadcasted_iota(jnp.int32, (up * north, up * north), 0)
    col = lax.broadcasted_iota(jnp.int32, (up * north, up * north), 1)
    return jnp.where(col == (row % up) * north + row // up, 1.0, 0.0).astype(BF)


def fill(features_ref, brick_ref, occupancy_ref, ext_ref):
    east, up, north = occupancy_ref.shape
    channels = features_ref.shape[2]
    bricks = brick_ref.shape[0]
    brick = lax.broadcasted_iota(jnp.int32, (east, north), 1) // (north // bricks)
    flags = jnp.zeros((east, north), jnp.int32)
    for b in range(bricks):
        flags = jnp.where(brick == b, brick_ref[b], flags)
    parts = [(occupancy_ref[:, u, :] * flags).astype(F32) for u in range(up)]
    wide = jnp.concatenate(parts, axis=1).astype(BF)
    mask = lax.dot_general(reorder(up, north), wide, NT, preferred_element_type=F32)
    rows = up * north
    lane = lax.broadcasted_iota(jnp.int32, (rows, 128 - channels), 1)
    for e in range(east):
        column = mask[:, e : e + 1]
        x = features_ref[e].astype(F32)
        kept = jnp.where(jnp.broadcast_to(column, x.shape) > 0, x, 0.0)
        spare = jnp.where(lane == 0, jnp.broadcast_to(column, lane.shape), 0.0)
        both = jnp.concatenate([kept, spare], axis=1)
        ext_ref[e + 2, 16 : 16 + rows] = both.astype(BF)


def main_kernel(
    features_ref, brick_ref, occupancy_ref, w1_hbm, w2_hbm, head_ref, teacher_ref,
    out_hbm, full1_hbm, full2_hbm,
    ext0_ref, ext2_ref, w1_ref, w2_ref, wf1, wf2, wb1, wb2, wide_head, flat_teacher, turned,
    cols0, cols1, cols2, acc, a1_ref, slope_ref, g1_ref, gt_ref, part_ref,
    packed1_ref, packed2_ref, out_ref,
    send0, recv0, send2, recv2, local, *rest,
):
    place = Place()
    devices = around() + place.peers()
    barrier = pltpu.get_barrier_semaphore()
    for device in devices:
        pl.semaphore_signal(barrier, inc=1, device_id=device, device_id_type=MESH)
    weights1 = pltpu.make_async_copy(w1_hbm, w1_ref, local.at[0])
    weights2 = pltpu.make_async_copy(w2_hbm, w2_ref, local.at[1])
    weights1.start()
    weights2.start()
    half = len(rest) // 2
    two = all_reduce(place, packed2_ref, *rest[:half])
    one = all_reduce(place, packed1_ref, *rest[half:])
    size_e, rows, channels = features_ref.shape
    classes = head_ref.shape[0]
    north = rows // 8
    wide = rows + 16

    fill(features_ref, brick_ref, occupancy_ref, ext0_ref)
    pl.semaphore_wait(barrier, len(devices))
    copies = exchange_start(ext0_ref, send0, recv0)
    wide_head[...] = jnp.zeros_like(wide_head)
    wide_head[0:classes, 0:channels] = head_ref[...]
    lay_teacher(teacher_ref, flat_teacher, turned)
    weights1.wait()
    lay_forward(w1_ref, wf1)
    lay_backward(w1_ref, wb1)
    weights2.wait()
    lay_forward(w2_ref, wf2)
    lay_backward(w2_ref, wb2)
    exchange_end(copies, ext0_ref)

    build(ext0_ref, 0, size_e + 4, 0, north + 2, cols1)
    convolve(cols1, wide, (size_e + 2) * wide, wf1, acc, True)

    def first(i, carry):
        at = pl.ds(pl.multiple_of(i * wide, 16), wide)
        x = ext0_ref[i + 1].astype(F32)[8 : 8 + wide]
        mask = jnp.broadcast_to(x[:, channels : channels + 1], (wide, 128))
        p1 = mask * acc[at]
        sig = jax.nn.sigmoid(p1)
        a1_ref[i] = (p1 * sig).astype(BF)
        slope_ref[at] = mask * slope_of(p1, sig)
        return carry

    lax.fori_loop(0, size_e + 2, first, 0)
    build(a1_ref, 0, size_e + 2, 0, north, cols2)
    convolve(cols2, rows, size_e * rows, wf2, acc, True)
    head = wide_head[...]
    row = lax.broadcasted_iota(jnp.int32, (128, 128), 0)
    col = lax.broadcasted_iota(jnp.int32, (128, 128), 1)

    def second(i, carry):
        at = pl.ds(pl.multiple_of(i * rows, 16), rows)
        x = ext0_ref[i + 2, 16 : 16 + rows].astype(F32)
        mask = jnp.broadcast_to(x[:, channels : channels + 1], (rows, 128))
        p2 = mask * acc[at]
        sig = jax.nn.sigmoid(p2)
        a2 = (p2 * sig).astype(BF)
        logits = lax.dot_general(a2, head, NT, preferred_element_type=F32)
        pick = jnp.where((row == col * size_e + i) & (col < classes), 1.0, 0.0).astype(BF)
        teacher = jnp.dot(turned[...], pick, preferred_element_type=F32)
        g = mask * (logits - teacher)
        high = g.astype(BF)
        left = g - high.astype(F32)
        mid = left.astype(BF)
        low = (left - mid.astype(F32)).astype(BF)
        back = jnp.dot(low, head, preferred_element_type=F32)
        back = back + jnp.dot(mid, head, preferred_element_type=F32)
        back = back + jnp.dot(high, head, preferred_element_type=F32)
        g2 = (mask * back * slope_of(p2, sig)).astype(BF)
        ext2_ref[i + 2, 16 : 16 + rows] = g2
        gt_ref[:, at] = g2.astype(F32).T.astype(BF)
        return carry

    lax.fori_loop(0, size_e, second, 0)
    copies = exchange_start(ext2_ref, send2, recv2)
    weight_grad(gt_ref, cols2, rows, part_ref)
    pack(part_ref, packed2_ref)
    next(two)
    build(ext0_ref, 1, size_e + 2, 1, north, cols0)
    exchange_end(copies, ext2_ref)
    next(two)
    build(ext2_ref, 0, size_e + 4, 0, north + 2, cols1)
    next(two)
    convolve(cols1, wide, (size_e + 2) * wide, wb2, acc, False)
    next(two)

    def third(i, carry):
        at = pl.ds(pl.multiple_of(i * wide, 16), wide)
        g1_ref[i] = (acc[at] * slope_ref[at]).astype(BF)
        return carry

    lax.fori_loop(0, size_e + 2, third, 0)

    def turn(i, carry):
        at = pl.ds(pl.multiple_of(i * rows, 16), rows)
        gt_ref[:, at] = g1_ref[i + 1].astype(F32)[8 : 8 + rows].T.astype(BF)
        return carry

    lax.fori_loop(0, size_e, turn, 0)
    weight_grad(gt_ref, cols0, rows, part_ref)
    pack(part_ref, packed1_ref)
    next(one)
    next(two)
    build(g1_ref, 0, size_e + 2, 0, north, cols2)
    next(one)
    next(two)
    convolve(cols2, rows, size_e * rows, wb1, acc, False)
    next(one)
    next(two)

    def last(i, carry):
        at = pl.ds(pl.multiple_of(i * rows, 16), rows)
        x = ext0_ref[i + 2, 16 : 16 + rows].astype(F32)
        mask = jnp.broadcast_to(x[:, channels : channels + 1], (rows, 128))
        out_ref[i] = (mask * acc[at])[:, 0:channels].astype(BF)
        return carry

    lax.fori_loop(0, size_e, last, 0)
    saved = pltpu.make_async_copy(out_ref, out_hbm, local.at[0])
    saved.start()
    next(one)
    next(two)
    put2 = pltpu.make_async_copy(rest[0], full2_hbm, local.at[1])
    put2.start()
    for _ in one:
        pass
    put1 = pltpu.make_async_copy(rest[half], full1_hbm, local.at[2])
    put1.start()
    saved.wait()
    put2.wait()
    put1.wait()


def finish_kernel(scale, out_ref, full1_ref, full2_ref, grad_features_ref, grad1_ref, grad2_ref):
    grad_features_ref[...] = out_ref[...]
    unpack(full1_ref, grad1_ref, scale)
    unpack(full2_ref, grad2_ref, scale)


def per_device(
    features, brick_active, voxel_occupancy, first_weights, second_weights, head, teacher
):
    channels, east, north, upward = features.shape
    classes = head.shape[0]
    rows = north * upward
    shape = jax.ShapeDtypeStruct
    sems = pltpu.SemaphoreType.DMA
    wide = rows + 16
    ext = VM((east + 4, rows + 32, 128), BF)
    field = VM((east + 2, wide, 128), BF)
    weights = VM(first_weights.shape, BF)
    forward, backward = VM((3, 128, 1152), BF), VM((3, 1152, 128), BF)
    narrow_cols = VM(((east + 2) * rows, 1152), BF)
    out = shape((east, rows, channels), BF)
    full = shape((PACKED, 128), BF)
    grad = shape((27, channels, channels), F32)
    vmem, anywhere = pl.BlockSpec(memory_space=VM), pl.BlockSpec(memory_space=pl.ANY)
    packed = VM((PACKED, 128), F32)
    result = pl.pallas_call(
        main_kernel,
        out_shape=(out, full, full),
        in_specs=[vmem, pl.BlockSpec(memory_space=pltpu.SMEM), vmem, anywhere, anywhere, vmem, vmem],
        out_specs=[anywhere] * 3,
        scratch_shapes=[
            ext, ext, weights, weights, forward, forward, backward, backward,
            VM((128, 128), BF),
            VM((classes * east * upward, north), F32),
            VM((128, 128), BF),
            narrow_cols, VM(((east + 4) * wide, 1152), BF), narrow_cols,
            VM(((east + 2) * wide, 128), F32),
            field,
            VM(((east + 2) * wide, 128), F32),
            field,
            VM((128, east * rows), BF),
            VM((27, channels, 128), F32),
            packed, packed,
            VM((east, rows, channels), BF),
            sems((8,)), sems((8,)), sems((8,)), sems((8,)), sems((3,)),
        ]
        + reduce_scratch(PACKED, lax.axis_size("east") // 4) * 2,
        compiler_params=pltpu.CompilerParams(
            collective_id=1, has_side_effects=True, vmem_limit_bytes=60 << 20
        ),
    )(
        features.transpose(1, 2, 3, 0).reshape(east, rows, channels),
        brick_active.reshape(-1),
        voxel_occupancy.transpose(0, 2, 1),
        first_weights,
        second_weights,
        head,
        teacher.transpose(0, 1, 3, 2),
    )
    total_voxels = lax.axis_size("east") * lax.axis_size("north") * east * north * upward
    scale = 1.0 / math.sqrt(total_voxels)
    grad_features, grad_first, grad_second = pl.pallas_call(
        functools.partial(finish_kernel, scale),
        out_shape=(out, grad, grad),
        in_specs=[vmem] * 3,
        out_specs=[vmem] * 3,
    )(*result)
    grad_features = grad_features.reshape(east, north, upward, channels).transpose(3, 0, 1, 2)
    return (grad_features, grad_first, grad_second)


def solution(mesh):
    in_specs = (
        P(None, "east", "north", None),
        P("east", "north", None),
        P("east", "north", None),
        P(),
        P(),
        P(),
        P(None, "east", "north", None),
    )
    out_specs = (P(None, "east", "north", None), P(), P())
    return jax.shard_map(
        per_device, mesh=mesh, in_specs=in_specs, out_specs=out_specs, check_vma=False
    )
```

```python
import functools
import math

import jax
import jax.numpy as jnp
from jax import lax
from jax.experimental import pallas as pl
from jax.experimental.pallas import tpu as pltpu
from jax.sharding import PartitionSpec as P

MESH = pl.DeviceIdType.MESH
VM = pltpu.VMEM
F32 = jnp.float32
BF = jnp.bfloat16
SIDES = tuple((a, b) for a in (-1, 0, 1) for b in (-1, 0, 1) if (a, b) != (0, 0))
NT = (((1,), (1,)), ((), ()))


def part(side, size):
    if side > 0:
        return size - 2, 2, 0
    if side < 0:
        return 0, 2, size + 2
    return 0, size, 2


def around():
    east, north = lax.axis_size("east"), lax.axis_size("north")
    e, n = lax.axis_index("east"), lax.axis_index("north")
    return [(lax.rem(e + a + east, east), lax.rem(n + b + north, north)) for a, b in SIDES]


def exchange_start(ext_ref, send, recv):
    size_e, size_n = ext_ref.shape[0] - 4, ext_ref.shape[1] // 8 - 4
    copies = []
    for i, (side, device) in enumerate(zip(SIDES, around())):
        se, le, de = part(side[0], size_e)
        sn, ln, dn = part(side[1], size_n)
        copy = pltpu.make_async_remote_copy(
            src_ref=ext_ref.at[pl.ds(se + 2, le), pl.ds((sn + 2) * 8, ln * 8)],
            dst_ref=ext_ref.at[pl.ds(de, le), pl.ds(dn * 8, ln * 8)],
            send_sem=send.at[i],
            recv_sem=recv.at[i],
            device_id=device,
            device_id_type=MESH,
        )
        copy.start()
        copies.append(copy)
    return copies


def exchange_end(copies, ext_ref):
    for copy in copies:
        copy.wait()
    e, n = lax.axis_index("east"), lax.axis_index("north")
    wide_e, wide_n, lanes = ext_ref.shape

    @pl.when(e == 0)
    def _():
        ext_ref[0:2] = jnp.zeros((2, wide_n, lanes), ext_ref.dtype)

    @pl.when(e == lax.axis_size("east") - 1)
    def _():
        ext_ref[wide_e - 2 : wide_e] = jnp.zeros((2, wide_n, lanes), ext_ref.dtype)

    @pl.when(n == 0)
    def _():
        ext_ref[:, 0:16] = jnp.zeros((wide_e, 16, lanes), ext_ref.dtype)

    @pl.when(n == lax.axis_size("north") - 1)
    def _():
        ext_ref[:, wide_n - 16 : wide_n] = jnp.zeros((wide_e, 16, lanes), ext_ref.dtype)


def build(src_ref, first, planes, start, count, out_ref):
    wide = src_ref.shape[1] // 8
    up = lax.broadcasted_iota(jnp.int32, (wide, 8, 128), 1)

    def body(i, carry):
        x = src_ref[first + i].astype(F32).reshape(wide, 8, 128)
        below = jnp.where(up == 0, 0.0, pltpu.roll(x, 1, 1))
        above = jnp.where(up == 7, 0.0, pltpu.roll(x, 7, 1))
        rows = pl.ds(pl.multiple_of(i * (count * 8), 16), count * 8)
        for dn in range(3):
            for du, piece in enumerate((below, x, above)):
                block = (dn * 3 + du) * 128
                y = piece[start + dn : start + dn + count].reshape(count * 8, 128)
                out_ref[rows, block : block + 128] = y.astype(BF)
        return carry

    lax.fori_loop(0, planes, body, 0)


def lay_forward(w_ref, out_ref):
    out_ref[...] = jnp.zeros_like(out_ref)
    size = w_ref.shape[1]
    for k in range(27):
        out_ref[k // 9, 0:size, (k % 9) * 128 : (k % 9) * 128 + size] = w_ref[k]


def lay_backward(w_ref, out_ref):
    out_ref[...] = jnp.zeros_like(out_ref)
    size = w_ref.shape[1]
    for k in range(27):
        out_ref[k // 9, (k % 9) * 128 : (k % 9) * 128 + size, 0:size] = w_ref[26 - k]


def convolve(x_ref, plane, rows, w_ref, acc_ref, transposed):
    acc_ref[0:rows] = jnp.zeros((rows, 128), F32)

    def body(i, carry):
        x = x_ref[pl.ds(pl.multiple_of(i * plane, 16), rows)]
        if transposed:
            y = lax.dot_general(x, w_ref[i], NT, preferred_element_type=F32)
        else:
            y = jnp.dot(x, w_ref[i], preferred_element_type=F32)
        acc_ref[0:rows] += y
        return carry

    lax.fori_loop(0, 3, body, 0)


def weight_grad(g_ref, x_ref, plane, out_ref):
    size = out_ref.shape[1]

    def body(i, carry):
        x = x_ref[pl.ds(pl.multiple_of(i * plane, 16), g_ref.shape[1])]
        y = jnp.dot(g_ref[...], x, preferred_element_type=F32)
        for b in range(9):
            out_ref[i * 9 + b] = y[0:size, b * 128 : (b + 1) * 128]
        return carry

    lax.fori_loop(0, 3, body, 0)


class Place:
    def __init__(self):
        e, n = lax.axis_index("east"), lax.axis_index("north")
        self.core = lax.rem(e, 2)
        self.z = lax.div(e, 4)
        self.zs = lax.axis_size("east") // 4
        self.xs = lax.axis_size("north") // 2
        self.x = lax.div(n, 2)
        self.y = lax.rem(lax.div(e, 2), 2) * 2 + lax.rem(n, 2)

    def device(self, core=None, x=None, y=None, z=None):
        core = self.core if core is None else core
        x = self.x if x is None else x
        y = self.y if y is None else y
        z = self.z if z is None else z
        return (z * 4 + lax.div(y, 2) * 2 + core, x * 2 + lax.rem(y, 2))

    def partner(self):
        return self.device(core=1 - self.core)

    def plane(self):
        steps = [(a, b) for a in range(self.xs) for b in range(4) if (a, b) != (0, 0)]
        steps.sort(key=lambda s: (min(s[0], self.xs - s[0]) + min(s[1], 4 - s[1]), s))
        found = []
        for a, b in steps:
            x, y = lax.rem(self.x + a, self.xs), lax.rem(self.y + b, 4)
            back = steps.index(((self.xs - a) % self.xs, (4 - b) % 4))
            found.append((x * 4 + y, self.device(x=x, y=y), back))
        return found

    def column(self):
        found = []
        for step in range(1, self.zs):
            found.append(self.device(z=lax.rem(self.z + step, self.zs)))
        return found

    def peers(self):
        return [self.partner()] + [device for _, device, _ in self.plane()] + self.column()


def all_reduce(place, src, full, away, got_core, held, got, slots, send, recv):
    half = src.shape[0] // 2
    plane = place.plane()
    piece = half // (len(plane) + 1)
    started = []

    def go(a, b, device):
        i = len(started)
        copy = pltpu.make_async_remote_copy(
            src_ref=a, dst_ref=b, send_sem=send.at[i], recv_sem=recv.at[i],
            device_id=device, device_id_type=MESH,
        )
        copy.start()
        started.append(copy)
        return copy

    def at(start, size):
        return pl.ds(pl.multiple_of(start, 64), size)

    mine = place.core * half
    theirs = (1 - place.core) * half

    def cast(i, carry):
        away[at(i * 256, 256)] = src[at(theirs + i * 256, 256)].astype(BF)
        return carry

    lax.fori_loop(0, half // 256, cast, 0)
    copies = [go(away, got_core, place.partner())]
    yield

    for copy in copies:
        copy.wait_recv()

    def pair(i, carry):
        total = src[at(mine + i * 256, 256)] + got_core[at(i * 256, 256)].astype(F32)
        held[at(i * 256, 256)] = total.astype(BF)
        return carry

    lax.fori_loop(0, half // 256, pair, 0)
    copies = []
    for i, (there, device, _) in enumerate(plane):
        copies.append(go(held.at[at(there * piece, piece)], got.at[i], device))
    yield

    own = (place.x * 4 + place.y) * piece
    total = src[at(mine + own, piece)] + got_core[at(own, piece)].astype(F32)
    for i, copy in enumerate(copies):
        copy.wait_recv()
        total = total + got[i].astype(F32)
    slots[place.z] = total.astype(BF)
    copies = []
    for device in place.column():
        copies.append(go(slots.at[place.z], slots.at[place.z], device))
    yield

    for copy in copies:
        copy.wait_recv()
    total = slots[0].astype(F32)
    for z in range(1, place.zs):
        total = total + slots[z].astype(F32)
    rows = at(mine + own, piece)
    full[rows] = total.astype(BF)
    copies = []
    for _, device, _ in plane:
        copies.append(go(full.at[rows], full.at[rows], device))
    last = [go(full.at[rows], full.at[rows], place.partner())]
    yield

    for copy, (_, _, back) in zip(copies, plane):
        copy.wait_recv()
        rows = at(mine + plane[back][0] * piece, piece)
        last.append(go(full.at[rows], full.at[rows], place.partner()))
    copies = last
    yield

    for copy in copies:
        copy.wait_recv()
    for copy in started:
        copy.wait_send()
    yield


REDUCE_COPIES = 56


def reduce_scratch(rows, places, zs):
    half = rows // 2
    piece = half // places
    return [
        VM((rows, 128), BF),
        VM((half, 128), BF),
        VM((half, 128), BF),
        VM((half, 128), BF),
        VM((places - 1, piece, 128), BF),
        VM((zs, piece, 128), BF),
        pltpu.SemaphoreType.DMA((REDUCE_COPIES,)),
        pltpu.SemaphoreType.DMA((REDUCE_COPIES,)),
    ]


PACKED = 2048


def pack(grad_ref, out_ref):
    size = grad_ref.shape[1]
    lane = lax.broadcasted_iota(jnp.int32, (size, 128), 1)

    def body(g, carry):
        spare = grad_ref[g * 4 + 3]
        for j in range(3):
            moved = pltpu.roll(spare, 96 - 32 * j, 1)
            rows = pl.ds(pl.multiple_of((g * 3 + j) * size, 32), size)
            out_ref[rows] = jnp.where(lane < 96, grad_ref[g * 4 + j], moved)
        return carry

    lax.fori_loop(0, 6, body, 0)
    for j in range(3):
        out_ref[(18 + j) * size : (19 + j) * size] = grad_ref[24 + j]
    out_ref[21 * size :] = jnp.zeros((out_ref.shape[0] - 21 * size, 128), F32)


def unpack(full_ref, out_ref, scale, out_hbm, sems):
    size = out_ref.shape[1]
    lane = lax.broadcasted_iota(jnp.int32, (size, 128), 1)
    copies = []

    def take(block):
        return full_ref[block * size : (block + 1) * size].astype(F32) * scale

    def put(start, count):
        part = pl.ds(start, count)
        copy = pltpu.make_async_copy(out_ref.at[part], out_hbm.at[part], sems.at[len(copies)])
        copy.start()
        copies.append(copy)

    for g in range(6):
        spare = []
        for j in range(3):
            value = take(g * 3 + j)
            out_ref[g * 4 + j] = value[:, 0:size]
            spare.append(pltpu.roll(value, 32 + 32 * j, 1))
        value = jnp.where(lane < 32, spare[0], jnp.where(lane < 64, spare[1], spare[2]))
        out_ref[g * 4 + 3] = value[:, 0:size]
        put(g * 4, 4)
    for j in range(3):
        out_ref[24 + j] = take(18 + j)[:, 0:size]
    put(24, 3)
    return copies


def slope_of(value, sig):
    return sig * (1.0 + value * (1.0 - sig))


def lay_teacher(teacher_ref, flat_ref, out_ref):
    classes, east, up, north = teacher_ref.shape
    flat_ref[...] = teacher_ref[...].astype(F32).reshape(flat_ref.shape)
    rows = classes * east
    parts = [flat_ref[pl.ds(u, rows, stride=up), :] for u in range(up)]
    wide = jnp.concatenate(parts, axis=1).astype(BF)
    wide = jnp.concatenate([wide, jnp.zeros((128 - rows, 128), BF)], axis=0)
    turned = lax.dot_general(reorder(up, north), wide, NT, preferred_element_type=F32)
    out_ref[...] = turned.astype(BF)


def reorder(up, north):
    row = lax.broadcasted_iota(jnp.int32, (up * north, up * north), 0)
    col = lax.broadcasted_iota(jnp.int32, (up * north, up * north), 1)
    return jnp.where(col == (row % up) * north + row // up, 1.0, 0.0).astype(BF)


def fill(features_ref, brick_ref, occupancy_ref, ext_ref):
    east, up, north = occupancy_ref.shape
    channels = features_ref.shape[2]
    bricks = brick_ref.shape[0]
    brick = lax.broadcasted_iota(jnp.int32, (east, north), 1) // (north // bricks)
    flags = jnp.zeros((east, north), jnp.int32)
    for b in range(bricks):
        flags = jnp.where(brick == b, brick_ref[b], flags)
    parts = [(occupancy_ref[:, u, :] * flags).astype(F32) for u in range(up)]
    wide = jnp.concatenate(parts, axis=1).astype(BF)
    mask = lax.dot_general(reorder(up, north), wide, NT, preferred_element_type=F32)
    rows = up * north
    lane = lax.broadcasted_iota(jnp.int32, (rows, 128 - channels), 1)
    for e in range(east):
        column = mask[:, e : e + 1]
        x = features_ref[e].astype(F32)
        kept = jnp.where(jnp.broadcast_to(column, x.shape) > 0, x, 0.0)
        spare = jnp.where(lane == 0, jnp.broadcast_to(column, lane.shape), 0.0)
        both = jnp.concatenate([kept, spare], axis=1)
        ext_ref[e + 2, 16 : 16 + rows] = both.astype(BF)


def main_kernel(
    features_hbm, brick_ref, occupancy_hbm, w1_hbm, w2_hbm, head_ref, teacher_hbm,
    out_hbm, full1_hbm, full2_hbm,
    ext0_ref, ext2_ref, w1_ref, w2_ref, wf1, wf2, wb1, wb2, wide_head, flat_teacher, turned,
    cols0, cols1, cols2, acc, a1_ref, slope_ref, g1_ref, gt_ref, part_ref,
    packed1_ref, packed2_ref, out_ref, features_ref, occupancy_ref, teacher_ref,
    send0, recv0, send2, recv2, local, *rest,
):
    place = Place()
    devices = around() + place.peers()
    barrier = pltpu.get_barrier_semaphore()
    for device in devices:
        pl.semaphore_signal(barrier, inc=1, device_id=device, device_id_type=MESH)
    pairs = (
        (features_hbm, features_ref), (occupancy_hbm, occupancy_ref),
        (w1_hbm, w1_ref), (w2_hbm, w2_ref), (teacher_hbm, teacher_ref),
    )
    loads = [pltpu.make_async_copy(a, b, local.at[3 + i]) for i, (a, b) in enumerate(pairs)]
    for load in loads:
        load.start()
    half = len(rest) // 2
    two = all_reduce(place, packed2_ref, *rest[:half])
    one = all_reduce(place, packed1_ref, *rest[half:])
    size_e, rows, channels = features_ref.shape
    classes = head_ref.shape[0]
    north = rows // 8
    wide = rows + 16

    loads[0].wait()
    loads[1].wait()
    fill(features_ref, brick_ref, occupancy_ref, ext0_ref)
    pl.semaphore_wait(barrier, len(devices))
    copies = exchange_start(ext0_ref, send0, recv0)
    wide_head[...] = jnp.zeros_like(wide_head)
    wide_head[0:classes, 0:channels] = head_ref[...]
    loads[4].wait()
    lay_teacher(teacher_ref, flat_teacher, turned)
    loads[2].wait()
    lay_forward(w1_ref, wf1)
    lay_backward(w1_ref, wb1)
    loads[3].wait()
    lay_forward(w2_ref, wf2)
    lay_backward(w2_ref, wb2)
    exchange_end(copies, ext0_ref)

    build(ext0_ref, 0, size_e + 4, 0, north + 2, cols1)
    convolve(cols1, wide, (size_e + 2) * wide, wf1, acc, True)

    def first(i, carry):
        at = pl.ds(pl.multiple_of(i * wide, 16), wide)
        x = ext0_ref[i + 1].astype(F32)[8 : 8 + wide]
        mask = jnp.broadcast_to(x[:, channels : channels + 1], (wide, 128))
        p1 = mask * acc[at]
        sig = jax.nn.sigmoid(p1)
        a1_ref[i] = (p1 * sig).astype(BF)
        slope_ref[at] = mask * slope_of(p1, sig)
        return carry

    lax.fori_loop(0, size_e + 2, first, 0)
    build(a1_ref, 0, size_e + 2, 0, north, cols2)
    convolve(cols2, rows, size_e * rows, wf2, acc, True)
    head = wide_head[...]
    row = lax.broadcasted_iota(jnp.int32, (128, 128), 0)
    col = lax.broadcasted_iota(jnp.int32, (128, 128), 1)

    group = 4

    def second(i, carry):
        planes = pl.ds(i * group + 2, group)
        at = pl.ds(pl.multiple_of(i * (group * rows), 128), group * rows)
        x = ext0_ref[planes, 16 : 16 + rows].astype(F32).reshape(group * rows, 128)
        mask = jnp.broadcast_to(x[:, channels : channels + 1], (group * rows, 128))
        p2 = mask * acc[at]
        sig = jax.nn.sigmoid(p2)
        a2 = (p2 * sig).astype(BF)
        logits = lax.dot_general(a2, head, NT, preferred_element_type=F32)
        teacher = []
        for b in range(group):
            pick = (row == col * size_e + (i * group + b)) & (col < classes)
            pick = jnp.where(pick, 1.0, 0.0).astype(BF)
            teacher.append(jnp.dot(turned[...], pick, preferred_element_type=F32))
        g = mask * (logits - jnp.concatenate(teacher, axis=0))
        high = g.astype(BF)
        left = g - high.astype(F32)
        mid = left.astype(BF)
        low = (left - mid.astype(F32)).astype(BF)
        back = jnp.dot(low, head, preferred_element_type=F32)
        back = back + jnp.dot(mid, head, preferred_element_type=F32)
        back = back + jnp.dot(high, head, preferred_element_type=F32)
        g2 = (mask * back * slope_of(p2, sig)).astype(BF)
        ext2_ref[planes, 16 : 16 + rows] = g2.reshape(group, rows, 128)
        gt_ref[:, at] = g2.astype(F32).T.astype(BF)
        return carry

    lax.fori_loop(0, size_e // group, second, 0)
    copies = exchange_start(ext2_ref, send2, recv2)
    weight_grad(gt_ref, cols2, rows, part_ref)
    pack(part_ref, packed2_ref)
    next(two)
    build(ext0_ref, 1, size_e + 2, 1, north, cols0)
    next(two)
    exchange_end(copies, ext2_ref)
    build(ext2_ref, 0, size_e + 4, 0, north + 2, cols1)
    convolve(cols1, wide, (size_e + 2) * wide, wb2, acc, False)
    next(two)

    def third(i, carry):
        at = pl.ds(pl.multiple_of(i * wide, 16), wide)
        g1_ref[i] = (acc[at] * slope_ref[at]).astype(BF)
        return carry

    lax.fori_loop(0, size_e + 2, third, 0)

    def turn(i, carry):
        at = pl.ds(pl.multiple_of(i * rows, 16), rows)
        gt_ref[:, at] = g1_ref[i + 1].astype(F32)[8 : 8 + rows].T.astype(BF)
        return carry

    lax.fori_loop(0, size_e, turn, 0)
    weight_grad(gt_ref, cols0, rows, part_ref)
    pack(part_ref, packed1_ref)
    next(one)
    build(g1_ref, 0, size_e + 2, 0, north, cols2)
    next(one)
    next(two)
    convolve(cols2, rows, size_e * rows, wb1, acc, False)

    def last(i, carry):
        at = pl.ds(pl.multiple_of(i * rows, 16), rows)
        x = ext0_ref[i + 2, 16 : 16 + rows].astype(F32)
        mask = jnp.broadcast_to(x[:, channels : channels + 1], (rows, 128))
        out_ref[i] = (mask * acc[at])[:, 0:channels].astype(BF)
        return carry

    lax.fori_loop(0, size_e, last, 0)
    saved = pltpu.make_async_copy(out_ref, out_hbm, local.at[0])
    saved.start()
    next(one)
    next(two)
    next(one)
    next(two)
    put2 = pltpu.make_async_copy(rest[0], full2_hbm, local.at[1])
    put2.start()
    next(one)
    next(one)
    put1 = pltpu.make_async_copy(rest[half], full1_hbm, local.at[2])
    put1.start()
    saved.wait()
    put2.wait()
    put1.wait()


def finish_kernel(
    scale, out_in, full1_in, full2_in, out_hbm, grad1_hbm, grad2_hbm,
    out_ref, full1_ref, full2_ref, grad1_ref, grad2_ref, loads, stores1, stores2,
):
    pairs = ((full2_in, full2_ref), (full1_in, full1_ref), (out_in, out_ref))
    copies = [pltpu.make_async_copy(a, b, loads.at[i]) for i, (a, b) in enumerate(pairs)]
    for copy in copies:
        copy.start()
    copies[0].wait()
    stores = unpack(full2_ref, grad2_ref, scale, grad2_hbm, stores2)
    copies[1].wait()
    stores += unpack(full1_ref, grad1_ref, scale, grad1_hbm, stores1)
    copies[2].wait()
    saved = pltpu.make_async_copy(out_ref, out_hbm, loads.at[3])
    saved.start()
    for copy in stores + [saved]:
        copy.wait()


def per_device(
    features, brick_active, voxel_occupancy, first_weights, second_weights, head, teacher
):
    channels, east, north, upward = features.shape
    classes = head.shape[0]
    rows = north * upward
    shape = jax.ShapeDtypeStruct
    sems = pltpu.SemaphoreType.DMA
    wide = rows + 16
    ext = VM((east + 4, rows + 32, 128), BF)
    field = VM((east + 2, wide, 128), BF)
    weights = VM(first_weights.shape, BF)
    forward, backward = VM((3, 128, 1152), BF), VM((3, 1152, 128), BF)
    narrow_cols = VM(((east + 2) * rows, 1152), BF)
    out = shape((east, rows, channels), BF)
    full = shape((PACKED, 128), BF)
    grad = shape((27, channels, channels), F32)
    vmem, anywhere = pl.BlockSpec(memory_space=VM), pl.BlockSpec(memory_space=pl.ANY)
    packed = VM((PACKED, 128), F32)
    result = pl.pallas_call(
        main_kernel,
        out_shape=(out, full, full),
        in_specs=[anywhere, pl.BlockSpec(memory_space=pltpu.SMEM), anywhere, anywhere, anywhere, vmem, anywhere],
        out_specs=[anywhere] * 3,
        scratch_shapes=[
            ext, ext, weights, weights, forward, forward, backward, backward,
            VM((128, 128), BF),
            VM((classes * east * upward, north), F32),
            VM((128, 128), BF),
            narrow_cols, VM(((east + 4) * wide, 1152), BF), narrow_cols,
            VM(((east + 2) * wide, 128), F32),
            field,
            VM(((east + 2) * wide, 128), F32),
            field,
            VM((128, east * rows), BF),
            VM((27, channels, 128), F32),
            packed, packed,
            VM((east, rows, channels), BF),
            VM((east, rows, channels), BF),
            VM((east, upward, north), jnp.int32),
            VM(head.shape[:1] + (east, upward, north), BF),
            sems((8,)), sems((8,)), sems((8,)), sems((8,)), sems((8,)),
        ]
        + reduce_scratch(PACKED, lax.axis_size("north") * 2, lax.axis_size("east") // 4) * 2,
        compiler_params=pltpu.CompilerParams(
            collective_id=1, has_side_effects=True, vmem_limit_bytes=60 << 20
        ),
    )(
        features.transpose(1, 2, 3, 0).reshape(east, rows, channels),
        brick_active.reshape(-1),
        voxel_occupancy.transpose(0, 2, 1),
        first_weights,
        second_weights,
        head,
        teacher.transpose(0, 1, 3, 2),
    )
    total_voxels = lax.axis_size("east") * lax.axis_size("north") * east * north * upward
    scale = 1.0 / math.sqrt(total_voxels)
    grad_features, grad_first, grad_second = pl.pallas_call(
        functools.partial(finish_kernel, scale),
        out_shape=(out, grad, grad),
        in_specs=[anywhere] * 3,
        out_specs=[anywhere] * 3,
        scratch_shapes=[VM(a.shape, a.dtype) for a in (out, full, full, grad, grad)]
        + [sems((4,)), sems((7,)), sems((7,))],
        compiler_params=pltpu.CompilerParams(vmem_limit_bytes=60 << 20),
    )(*result)
    grad_features = grad_features.reshape(east, north, upward, channels).transpose(3, 0, 1, 2)
    return (grad_features, grad_first, grad_second)


def solution(mesh):
    in_specs = (
        P(None, "east", "north", None),
        P("east", "north", None),
        P("east", "north", None),
        P(),
        P(),
        P(),
        P(None, "east", "north", None),
    )
    out_specs = (P(None, "east", "north", None), P(), P())
    return jax.shard_map(
        per_device, mesh=mesh, in_specs=in_specs, out_specs=out_specs, check_vma=False
    )
```

```python
import functools
import math

import jax
import jax.numpy as jnp
from jax import lax
from jax.experimental import pallas as pl
from jax.experimental.pallas import tpu as pltpu
from jax.sharding import PartitionSpec as P

MESH = pl.DeviceIdType.MESH
VM = pltpu.VMEM
F32 = jnp.float32
BF = jnp.bfloat16
SIDES = ((-1, -1), (-1, 1), (1, -1), (1, 1), (-1, 0), (1, 0), (0, -1), (0, 1))
NT = (((1,), (1,)), ((), ()))


def part(side, size):
    if side > 0:
        return size - 2, 2, 0
    if side < 0:
        return 0, 2, size + 2
    return 0, size, 2


def around():
    east, north = lax.axis_size("east"), lax.axis_size("north")
    e, n = lax.axis_index("east"), lax.axis_index("north")
    return [(lax.rem(e + a + east, east), lax.rem(n + b + north, north)) for a, b in SIDES]


def exchange_start(x_ref, ext_ref, send, recv):
    size_e, size_n = ext_ref.shape[0] - 4, ext_ref.shape[1] // 8 - 4
    copies = []
    for i, (side, device) in enumerate(zip(SIDES, around())):
        se, le, de = part(side[0], size_e)
        sn, ln, dn = part(side[1], size_n)
        copy = pltpu.make_async_remote_copy(
            src_ref=x_ref.at[pl.ds(se + 2, le), pl.ds((sn + 2) * 8, ln * 8)],
            dst_ref=ext_ref.at[pl.ds(de, le), pl.ds(dn * 8, ln * 8)],
            send_sem=send.at[i],
            recv_sem=recv.at[i],
            device_id=device,
            device_id_type=MESH,
        )
        copy.start()
        copies.append(copy)
    return copies


def exchange_end(copies, ext_ref):
    for copy in copies:
        copy.wait()
    e, n = lax.axis_index("east"), lax.axis_index("north")
    wide_e, wide_n, lanes = ext_ref.shape

    @pl.when(e == 0)
    def _():
        ext_ref[0:2] = jnp.zeros((2, wide_n, lanes), ext_ref.dtype)

    @pl.when(e == lax.axis_size("east") - 1)
    def _():
        ext_ref[wide_e - 2 : wide_e] = jnp.zeros((2, wide_n, lanes), ext_ref.dtype)

    @pl.when(n == 0)
    def _():
        ext_ref[:, 0:16] = jnp.zeros((wide_e, 16, lanes), ext_ref.dtype)

    @pl.when(n == lax.axis_size("north") - 1)
    def _():
        ext_ref[:, wide_n - 16 : wide_n] = jnp.zeros((wide_e, 16, lanes), ext_ref.dtype)


def build(src_ref, first, planes, start, count, out_ref):
    wide = src_ref.shape[1] // 8
    up = lax.broadcasted_iota(jnp.int32, (wide, 8, 128), 1)

    def body(i, carry):
        x = src_ref[first + i].astype(F32).reshape(wide, 8, 128)
        below = jnp.where(up == 0, 0.0, pltpu.roll(x, 1, 1))
        above = jnp.where(up == 7, 0.0, pltpu.roll(x, 7, 1))
        rows = pl.ds(pl.multiple_of(i * (count * 8), 16), count * 8)
        for dn in range(3):
            for du, piece in enumerate((below, x, above)):
                block = (dn * 3 + du) * 128
                y = piece[start + dn : start + dn + count].reshape(count * 8, 128)
                out_ref[rows, block : block + 128] = y.astype(BF)
        return carry

    lax.fori_loop(0, planes, body, 0)


def lay_forward(w_ref, out_ref):
    out_ref[...] = jnp.zeros_like(out_ref)
    size = w_ref.shape[1]
    for k in range(27):
        out_ref[k // 9, 0:size, (k % 9) * 128 : (k % 9) * 128 + size] = w_ref[k]


def lay_backward(w_ref, out_ref):
    out_ref[...] = jnp.zeros_like(out_ref)
    size = w_ref.shape[1]
    for k in range(27):
        out_ref[k // 9, (k % 9) * 128 : (k % 9) * 128 + size, 0:size] = w_ref[26 - k]


def product(x, w, transposed):
    if transposed:
        return lax.dot_general(x, w, NT, preferred_element_type=F32)
    return jnp.dot(x, w, preferred_element_type=F32)


def convolve(x_ref, plane, rows, w_ref, acc_ref, transposed):
    total = product(x_ref[0:rows], w_ref[0], transposed)
    for i in (1, 2):
        total = total + product(x_ref[i * plane : i * plane + rows], w_ref[i], transposed)
    acc_ref[0:rows] = total


def build_halo(ext_ref, out_ref):
    planes, rows = ext_ref.shape[0], ext_ref.shape[1] - 16
    inner = planes - 4
    build(ext_ref, 0, 2, 0, rows // 8, out_ref.at[0 : 2 * rows])
    build(ext_ref, planes - 2, 2, 0, rows // 8, out_ref.at[2 * rows + 32 * inner :])
    wide = ext_ref.shape[1] // 8
    up = lax.broadcasted_iota(jnp.int32, (4, 8, 128), 1)
    zero = jnp.zeros((2, 8, 128), F32)

    def body(i, carry):
        x = ext_ref[i + 2].astype(F32).reshape(wide, 8, 128)
        x = jnp.concatenate([x[0:2], x[wide - 2 :]], axis=0)
        below = jnp.where(up == 0, 0.0, pltpu.roll(x, 1, 1))
        above = jnp.where(up == 7, 0.0, pltpu.roll(x, 7, 1))
        at = pl.ds(pl.multiple_of(2 * rows + i * 32, 16), 32)
        for dn in range(3):
            for du, piece in enumerate((below, x, above)):
                block = (dn * 3 + du) * 128
                low = jnp.concatenate([piece[0:2], zero], axis=0)[dn : dn + 2]
                high = jnp.concatenate([zero, piece[2:4]], axis=0)[dn : dn + 2]
                y = jnp.concatenate([low, high], axis=0).reshape(32, 128)
                out_ref[at, block : block + 128] = y.astype(BF)
        return carry

    lax.fori_loop(0, inner, body, 0)


def convolve_halo(x_ref, plane, inner, w_ref, acc_ref, transposed):
    count = 2 * plane + 32 * inner
    last = inner + 1
    for i in range(3):
        y = product(x_ref[i * plane : i * plane + count], w_ref[i], transposed)
        before = (2 - i) * plane
        if before:
            acc_ref[0:before] += y[0:before]
        if i:
            start = (last + 1 - i) * plane
            acc_ref[start : start + i * plane] += y[count - i * plane :]
        for e in range(inner):
            at = (e + 2 - i) * plane
            part = before + e * 32
            acc_ref[at : at + 16] += y[part : part + 16]
            acc_ref[at + plane - 16 : at + plane] += y[part + 16 : part + 32]


def weight_grad(g_ref, x_ref, plane, out_ref, begin=0, end=3):
    size = out_ref.shape[1]

    def body(i, carry):
        x = x_ref[pl.ds(pl.multiple_of(i * plane, 16), g_ref.shape[1])]
        y = jnp.dot(g_ref[...], x, preferred_element_type=F32)
        for b in range(9):
            out_ref[i * 9 + b] = y[0:size, b * 128 : (b + 1) * 128]
        return carry

    lax.fori_loop(0, 3, body, 0)


class Place:
    def __init__(self):
        e, n = lax.axis_index("east"), lax.axis_index("north")
        self.core = lax.rem(e, 2)
        self.z = lax.div(e, 4)
        self.zs = lax.axis_size("east") // 4
        self.xs = lax.axis_size("north") // 2
        self.x = lax.div(n, 2)
        self.y = lax.rem(lax.div(e, 2), 2) * 2 + lax.rem(n, 2)

    def device(self, core=None, x=None, y=None, z=None):
        core = self.core if core is None else core
        x = self.x if x is None else x
        y = self.y if y is None else y
        z = self.z if z is None else z
        return (z * 4 + lax.div(y, 2) * 2 + core, x * 2 + lax.rem(y, 2))

    def partner(self):
        return self.device(core=1 - self.core)

    def plane(self):
        steps = [(a, b) for a in range(self.xs) for b in range(4) if (a, b) != (0, 0)]
        steps.sort(key=lambda s: (min(s[0], self.xs - s[0]) + min(s[1], 4 - s[1]), s))
        found = []
        for a, b in steps:
            x, y = lax.rem(self.x + a, self.xs), lax.rem(self.y + b, 4)
            back = steps.index(((self.xs - a) % self.xs, (4 - b) % 4))
            found.append((x * 4 + y, self.device(x=x, y=y), back))
        return found

    def column(self):
        found = []
        for step in range(1, self.zs):
            found.append(self.device(z=lax.rem(self.z + step, self.zs)))
        return found

    def peers(self):
        return [self.partner()] + [device for _, device, _ in self.plane()] + self.column()


def all_reduce(place, src, full, away, got_core, held, got, slots, send, recv):
    half = src.shape[0] // 2
    plane = place.plane()
    piece = half // (len(plane) + 1)
    started = []

    def go(a, b, device):
        i = len(started)
        copy = pltpu.make_async_remote_copy(
            src_ref=a, dst_ref=b, send_sem=send.at[i], recv_sem=recv.at[i],
            device_id=device, device_id_type=MESH,
        )
        copy.start()
        started.append(copy)
        return copy

    def at(start, size):
        return pl.ds(pl.multiple_of(start, 32), size)

    mine = place.core * half
    theirs = (1 - place.core) * half

    def cast(i, carry):
        away[at(i * 256, 256)] = src[at(theirs + i * 256, 256)].astype(BF)
        return carry

    lax.fori_loop(0, half // 256, cast, 0)
    copies = [go(away, got_core, place.partner())]
    yield

    for copy in copies:
        copy.wait_recv()

    def pair(i, carry):
        total = src[at(mine + i * 256, 256)] + got_core[at(i * 256, 256)].astype(F32)
        held[at(i * 256, 256)] = total.astype(BF)
        return carry

    lax.fori_loop(0, half // 256, pair, 0)
    copies = []
    for i, (there, device, _) in enumerate(plane):
        copies.append(go(held.at[at(there * piece, piece)], got.at[i], device))
    yield

    own = (place.x * 4 + place.y) * piece
    total = src[at(mine + own, piece)] + got_core[at(own, piece)].astype(F32)
    for i, copy in enumerate(copies):
        copy.wait_recv()
        total = total + got[i].astype(F32)
    slots[place.z] = total.astype(BF)
    copies = []
    for device in place.column():
        copies.append(go(slots.at[place.z], slots.at[place.z], device))
    yield

    for copy in copies:
        copy.wait_recv()
    total = slots[0].astype(F32)
    for z in range(1, place.zs):
        total = total + slots[z].astype(F32)
    rows = at(mine + own, piece)
    full[rows] = total.astype(BF)
    copies = []
    for _, device, _ in plane:
        copies.append(go(full.at[rows], full.at[rows], device))
    last = [go(full.at[rows], full.at[rows], place.partner())]
    yield

    for copy, (_, _, back) in zip(copies, plane):
        copy.wait_recv()
        rows = at(mine + plane[back][0] * piece, piece)
        last.append(go(full.at[rows], full.at[rows], place.partner()))
    copies = last
    yield

    for copy in copies:
        copy.wait_recv()
    for copy in started:
        copy.wait_send()
    yield


REDUCE_COPIES = 56


def reduce_scratch(rows, places, zs):
    half = rows // 2
    piece = half // places
    return [
        VM((rows, 128), BF),
        VM((half, 128), BF),
        VM((half, 128), BF),
        VM((half, 128), BF),
        VM((places - 1, piece, 128), BF),
        VM((zs, piece, 128), BF),
        pltpu.SemaphoreType.DMA((REDUCE_COPIES,)),
        pltpu.SemaphoreType.DMA((REDUCE_COPIES,)),
    ]


PACKED = 2048


def pack(grad_ref, out_ref, begin=0, end=6):
    size = grad_ref.shape[1]
    lane = lax.broadcasted_iota(jnp.int32, (size, 128), 1)

    def body(g, carry):
        spare = grad_ref[g * 4 + 3]
        for j in range(3):
            moved = pltpu.roll(spare, 96 - 32 * j, 1)
            rows = pl.ds(pl.multiple_of((g * 3 + j) * size, 32), size)
            out_ref[rows] = jnp.where(lane < 96, grad_ref[g * 4 + j], moved)
        return carry

    lax.fori_loop(begin, end, body, 0)
    if end < 6:
        return
    for j in range(3):
        out_ref[(18 + j) * size : (19 + j) * size] = grad_ref[24 + j]
    out_ref[21 * size :] = jnp.zeros((out_ref.shape[0] - 21 * size, 128), F32)


def unpack(full_ref, out_ref, scale, out_hbm, sems):
    size = out_ref.shape[1]
    lane = lax.broadcasted_iota(jnp.int32, (size, 128), 1)
    copies = []

    def take(block):
        return full_ref[block * size : (block + 1) * size].astype(F32) * scale

    def put(start, count):
        part = pl.ds(start, count)
        copy = pltpu.make_async_copy(out_ref.at[part], out_hbm.at[part], sems.at[len(copies)])
        copy.start()
        copies.append(copy)

    for g in range(6):
        spare = []
        for j in range(3):
            value = take(g * 3 + j)
            out_ref[g * 4 + j] = value[:, 0:size]
            spare.append(pltpu.roll(value, 32 + 32 * j, 1))
        value = jnp.where(lane < 32, spare[0], jnp.where(lane < 64, spare[1], spare[2]))
        out_ref[g * 4 + 3] = value[:, 0:size]
        put(g * 4, 4)
    for j in range(3):
        out_ref[24 + j] = take(18 + j)[:, 0:size]
    put(24, 3)
    return copies


def slope_of(value, sig):
    return sig * (1.0 + value * (1.0 - sig))


def lay_teacher(teacher_ref, flat_ref, out_ref):
    classes, east, up, north = teacher_ref.shape
    flat_ref[...] = teacher_ref[...].astype(F32).reshape(flat_ref.shape)
    rows = classes * east
    parts = [flat_ref[pl.ds(u, rows, stride=up), :] for u in range(up)]
    wide = jnp.concatenate(parts, axis=1).astype(BF)
    wide = jnp.concatenate([wide, jnp.zeros((128 - rows, 128), BF)], axis=0)
    turned = lax.dot_general(reorder(up, north), wide, NT, preferred_element_type=F32)
    out_ref[...] = turned.astype(BF)


def reorder(up, north):
    row = lax.broadcasted_iota(jnp.int32, (up * north, up * north), 0)
    col = lax.broadcasted_iota(jnp.int32, (up * north, up * north), 1)
    return jnp.where(col == (row % up) * north + row // up, 1.0, 0.0).astype(BF)


def fill(features_ref, brick_ref, occupancy_ref, ext_ref, own_ref):
    east, up, north = occupancy_ref.shape
    channels = features_ref.shape[2]
    bricks = brick_ref.shape[0]
    brick = lax.broadcasted_iota(jnp.int32, (east, north), 1) // (north // bricks)
    flags = jnp.zeros((east, north), jnp.int32)
    for b in range(bricks):
        flags = jnp.where(brick == b, brick_ref[b], flags)
    parts = [(occupancy_ref[:, u, :] * flags).astype(F32) for u in range(up)]
    wide = jnp.concatenate(parts, axis=1).astype(BF)
    mask = lax.dot_general(reorder(up, north), wide, NT, preferred_element_type=F32)
    rows = up * north
    lane = lax.broadcasted_iota(jnp.int32, (rows, 128 - channels), 1)
    for e in range(east):
        column = mask[:, e : e + 1]
        x = features_ref[e].astype(F32)
        kept = jnp.where(jnp.broadcast_to(column, x.shape) > 0, x, 0.0)
        spare = jnp.where(lane == 0, jnp.broadcast_to(column, lane.shape), 0.0)
        both = jnp.concatenate([kept, spare], axis=1)
        ext_ref[e + 2, 16 : 16 + rows] = both.astype(BF)
        own_ref[e + 2, 16 : 16 + rows] = both.astype(BF)


def main_kernel(
    features_hbm, brick_ref, occupancy_hbm, w1_hbm, w2_hbm, head_ref, teacher_hbm,
    out_hbm, full1_hbm, full2_hbm,
    ext0_ref, own_ref, halo_cols, ext2_ref, w1_ref, w2_ref, wf1, wf2, wb1, wb2, wide_head, flat_teacher, turned,
    cols0, cols1, cols2, acc, a1_ref, slope_ref, g1_ref, gt_ref, part_ref,
    packed1_ref, packed2_ref, out_ref, features_ref, occupancy_ref, teacher_ref,
    send0, recv0, send2, recv2, local, *rest,
):
    place = Place()
    devices = around() + place.peers()
    barrier = pltpu.get_barrier_semaphore()
    for device in devices:
        pl.semaphore_signal(barrier, inc=1, device_id=device, device_id_type=MESH)
    pairs = (
        (features_hbm, features_ref), (occupancy_hbm, occupancy_ref),
        (w1_hbm, w1_ref), (w2_hbm, w2_ref), (teacher_hbm, teacher_ref),
    )
    loads = [pltpu.make_async_copy(a, b, local.at[3 + i]) for i, (a, b) in enumerate(pairs)]
    for load in loads:
        load.start()
    split = packed1_ref.shape[0] // 2
    two = all_reduce(place, packed2_ref, *rest[:8])
    one_a = all_reduce(place, packed1_ref.at[0:split], *rest[8:16])
    one_b = all_reduce(place, packed1_ref.at[split:], *rest[16:24])
    size_e, rows, channels = features_ref.shape
    classes = head_ref.shape[0]
    north = rows // 8
    wide = rows + 16

    loads[0].wait()
    loads[1].wait()
    fill(features_ref, brick_ref, occupancy_ref, ext0_ref, own_ref)
    pl.semaphore_wait(barrier, len(devices))
    copies = exchange_start(own_ref, ext0_ref, send0, recv0)
    edge = jnp.zeros((size_e + 4, 16, 128), BF)
    own_ref[:, 0:16] = edge
    own_ref[:, 16 + rows : 32 + rows] = edge
    cols1[0 : 2 * wide] = jnp.zeros((2 * wide, cols1.shape[1]), BF)
    cols1[(size_e + 2) * wide :] = jnp.zeros((2 * wide, cols1.shape[1]), BF)
    build(own_ref, 2, size_e, 0, north + 2, cols1.at[2 * wide : (size_e + 2) * wide])
    loads[2].wait()
    lay_forward(w1_ref, wf1)
    convolve(cols1, wide, (size_e + 2) * wide, wf1, acc, True)
    loads[3].wait()
    lay_forward(w2_ref, wf2)
    wide_head[...] = jnp.zeros_like(wide_head)
    wide_head[0:classes, 0:channels] = head_ref[...]
    loads[4].wait()
    lay_teacher(teacher_ref, flat_teacher, turned)
    exchange_end(copies, ext0_ref)
    build_halo(ext0_ref, halo_cols)
    convolve_halo(halo_cols, wide, size_e, wf1, acc, True)

    def first(i, carry):
        at = pl.ds(pl.multiple_of(i * wide, 16), wide)
        x = ext0_ref[i + 1].astype(F32)[8 : 8 + wide]
        mask = jnp.broadcast_to(x[:, channels : channels + 1], (wide, 128))
        p1 = mask * acc[at]
        sig = jax.nn.sigmoid(p1)
        a1_ref[i] = (p1 * sig).astype(BF)
        slope_ref[at] = mask * slope_of(p1, sig)
        return carry

    lax.fori_loop(0, size_e + 2, first, 0)
    build(a1_ref, 0, size_e + 2, 0, north, cols2)
    convolve(cols2, rows, size_e * rows, wf2, acc, True)
    head = wide_head[...]
    row = lax.broadcasted_iota(jnp.int32, (128, 128), 0)
    col = lax.broadcasted_iota(jnp.int32, (128, 128), 1)

    group = 4

    def second(i, carry):
        planes = pl.ds(i * group + 2, group)
        at = pl.ds(pl.multiple_of(i * (group * rows), 128), group * rows)
        x = ext0_ref[planes, 16 : 16 + rows].astype(F32).reshape(group * rows, 128)
        mask = jnp.broadcast_to(x[:, channels : channels + 1], (group * rows, 128))
        p2 = mask * acc[at]
        sig = jax.nn.sigmoid(p2)
        a2 = (p2 * sig).astype(BF)
        logits = lax.dot_general(a2, head, NT, preferred_element_type=F32)
        teacher = []
        for b in range(group):
            pick = (row == col * size_e + (i * group + b)) & (col < classes)
            pick = jnp.where(pick, 1.0, 0.0).astype(BF)
            teacher.append(jnp.dot(turned[...], pick, preferred_element_type=F32))
        g = mask * (logits - jnp.concatenate(teacher, axis=0))
        high = g.astype(BF)
        left = g - high.astype(F32)
        mid = left.astype(BF)
        low = (left - mid.astype(F32)).astype(BF)
        back = jnp.dot(low, head, preferred_element_type=F32)
        back = back + jnp.dot(mid, head, preferred_element_type=F32)
        back = back + jnp.dot(high, head, preferred_element_type=F32)
        g2 = (mask * back * slope_of(p2, sig)).astype(BF)
        ext2_ref[planes, 16 : 16 + rows] = g2.reshape(group, rows, 128)
        gt_ref[:, at] = g2.astype(F32).T.astype(BF)
        return carry

    lax.fori_loop(0, size_e // group, second, 0)
    copies = exchange_start(ext2_ref, ext2_ref, send2, recv2)
    weight_grad(gt_ref, cols2, rows, part_ref)
    pack(part_ref, packed2_ref)
    next(two)
    lay_backward(w2_ref, wb2)
    lay_backward(w1_ref, wb1)
    build(ext0_ref, 1, size_e + 2, 1, north, cols0)
    next(two)
    exchange_end(copies, ext2_ref)
    build(ext2_ref, 0, size_e + 4, 0, north + 2, cols1)
    convolve(cols1, wide, (size_e + 2) * wide, wb2, acc, False)
    next(two)

    def third(i, carry):
        at = pl.ds(pl.multiple_of(i * wide, 16), wide)
        g1_ref[i] = (acc[at] * slope_ref[at]).astype(BF)
        return carry

    lax.fori_loop(0, size_e + 2, third, 0)

    def turn(i, carry):
        at = pl.ds(pl.multiple_of(i * rows, 16), rows)
        gt_ref[:, at] = g1_ref[i + 1].astype(F32)[8 : 8 + rows].T.astype(BF)
        return carry

    lax.fori_loop(0, size_e, turn, 0)
    weight_grad(gt_ref, cols0, rows, part_ref, 0, 2)
    pack(part_ref, packed1_ref, 0, 4)
    next(one_a)
    weight_grad(gt_ref, cols0, rows, part_ref, 2, 3)
    pack(part_ref, packed1_ref, 4, 6)
    next(one_b)
    next(one_a)
    next(one_b)
    build(g1_ref, 0, size_e + 2, 0, north, cols2)
    next(two)
    convolve(cols2, rows, size_e * rows, wb1, acc, False)

    def last(i, carry):
        at = pl.ds(pl.multiple_of(i * rows, 16), rows)
        x = ext0_ref[i + 2, 16 : 16 + rows].astype(F32)
        mask = jnp.broadcast_to(x[:, channels : channels + 1], (rows, 128))
        out_ref[i] = (mask * acc[at])[:, 0:channels].astype(BF)
        return carry

    lax.fori_loop(0, size_e, last, 0)
    saved = pltpu.make_async_copy(out_ref, out_hbm, local.at[0])
    saved.start()
    next(one_a)
    next(one_b)
    next(two)
    next(one_a)
    next(one_b)
    next(two)
    put2 = pltpu.make_async_copy(rest[0], full2_hbm, local.at[1])
    put2.start()
    next(one_a)
    next(one_b)
    next(one_a)
    put1a = pltpu.make_async_copy(rest[8], full1_hbm.at[0:split], local.at[2])
    put1a.start()
    next(one_b)
    put1b = pltpu.make_async_copy(rest[16], full1_hbm.at[pl.ds(split, split)], local.at[3])
    put1b.start()
    saved.wait()
    put2.wait()
    put1a.wait()
    put1b.wait()


def finish_kernel(
    scale, out_in, full1_in, full2_in, out_hbm, grad1_hbm, grad2_hbm,
    out_ref, full1_ref, full2_ref, grad1_ref, grad2_ref, loads, stores1, stores2,
):
    pairs = ((full2_in, full2_ref), (full1_in, full1_ref), (out_in, out_ref))
    copies = [pltpu.make_async_copy(a, b, loads.at[i]) for i, (a, b) in enumerate(pairs)]
    for copy in copies:
        copy.start()
    copies[0].wait()
    stores = unpack(full2_ref, grad2_ref, scale, grad2_hbm, stores2)
    copies[1].wait()
    stores += unpack(full1_ref, grad1_ref, scale, grad1_hbm, stores1)
    copies[2].wait()
    saved = pltpu.make_async_copy(out_ref, out_hbm, loads.at[3])
    saved.start()
    for copy in stores + [saved]:
        copy.wait()


def per_device(
    features, brick_active, voxel_occupancy, first_weights, second_weights, head, teacher
):
    channels, east, north, upward = features.shape
    classes = head.shape[0]
    rows = north * upward
    shape = jax.ShapeDtypeStruct
    sems = pltpu.SemaphoreType.DMA
    wide = rows + 16
    ext = VM((east + 4, rows + 32, 128), BF)
    field = VM((east + 2, wide, 128), BF)
    weights = VM(first_weights.shape, BF)
    forward, backward = VM((3, 128, 1152), BF), VM((3, 1152, 128), BF)
    narrow_cols = VM(((east + 2) * rows, 1152), BF)
    out = shape((east, rows, channels), BF)
    full = shape((PACKED, 128), BF)
    grad = shape((27, channels, channels), F32)
    vmem, anywhere = pl.BlockSpec(memory_space=VM), pl.BlockSpec(memory_space=pl.ANY)
    packed = VM((PACKED, 128), F32)
    result = pl.pallas_call(
        main_kernel,
        out_shape=(out, full, full),
        in_specs=[anywhere, pl.BlockSpec(memory_space=pltpu.SMEM), anywhere, anywhere, anywhere, vmem, anywhere],
        out_specs=[anywhere] * 3,
        scratch_shapes=[
            ext, ext, VM((4 * wide + 32 * east, 1152), BF), ext, weights, weights, forward, forward, backward, backward,
            VM((128, 128), BF),
            VM((classes * east * upward, north), F32),
            VM((128, 128), BF),
            narrow_cols, VM(((east + 4) * wide, 1152), BF), narrow_cols,
            VM(((east + 2) * wide, 128), F32),
            field,
            VM(((east + 2) * wide, 128), F32),
            field,
            VM((128, east * rows), BF),
            VM((27, channels, 128), F32),
            packed, packed,
            VM((east, rows, channels), BF),
            VM((east, rows, channels), BF),
            VM((east, upward, north), jnp.int32),
            VM(head.shape[:1] + (east, upward, north), BF),
            sems((8,)), sems((8,)), sems((8,)), sems((8,)), sems((8,)),
        ]
        + [
            item
            for size in (PACKED, PACKED // 2, PACKED // 2)
            for item in reduce_scratch(size, lax.axis_size("north") * 2, lax.axis_size("east") // 4)
        ],
        compiler_params=pltpu.CompilerParams(
            collective_id=1, has_side_effects=True, vmem_limit_bytes=60 << 20
        ),
    )(
        features.transpose(1, 2, 3, 0).reshape(east, rows, channels),
        brick_active.reshape(-1),
        voxel_occupancy.transpose(0, 2, 1),
        first_weights,
        second_weights,
        head,
        teacher.transpose(0, 1, 3, 2),
    )
    total_voxels = lax.axis_size("east") * lax.axis_size("north") * east * north * upward
    scale = 1.0 / math.sqrt(total_voxels)
    grad_features, grad_first, grad_second = pl.pallas_call(
        functools.partial(finish_kernel, scale),
        out_shape=(out, grad, grad),
        in_specs=[anywhere] * 3,
        out_specs=[anywhere] * 3,
        scratch_shapes=[VM(a.shape, a.dtype) for a in (out, full, full, grad, grad)]
        + [sems((4,)), sems((7,)), sems((7,))],
        compiler_params=pltpu.CompilerParams(vmem_limit_bytes=60 << 20),
    )(*result)
    grad_features = grad_features.reshape(east, north, upward, channels).transpose(3, 0, 1, 2)
    return (grad_features, grad_first, grad_second)


def solution(mesh):
    in_specs = (
        P(None, "east", "north", None),
        P("east", "north", None),
        P("east", "north", None),
        P(),
        P(),
        P(),
        P(None, "east", "north", None),
    )
    out_specs = (P(None, "east", "north", None), P(), P())
    return jax.shard_map(
        per_device, mesh=mesh, in_specs=in_specs, out_specs=out_specs, check_vma=False
    )
```

```python
import functools
import math

import jax
import jax.numpy as jnp
from jax import lax
from jax.experimental import pallas as pl
from jax.experimental.pallas import tpu as pltpu
from jax.sharding import PartitionSpec as P

MESH = pl.DeviceIdType.MESH
VM = pltpu.VMEM
F32 = jnp.float32
BF = jnp.bfloat16
SIDES = ((-1, -1), (-1, 1), (1, -1), (1, 1), (-1, 0), (1, 0), (0, -1), (0, 1))
NT = (((1,), (1,)), ((), ()))


def part(side, size):
    if side > 0:
        return size - 2, 2, 0
    if side < 0:
        return 0, 2, size + 2
    return 0, size, 2


def around():
    east, north = lax.axis_size("east"), lax.axis_size("north")
    e, n = lax.axis_index("east"), lax.axis_index("north")
    return [(lax.rem(e + a + east, east), lax.rem(n + b + north, north)) for a, b in SIDES]


def exchange_start(x_ref, ext_ref, send, recv):
    size_e, size_n = ext_ref.shape[0] - 4, ext_ref.shape[1] // 8 - 4
    copies = []
    for i, (side, device) in enumerate(zip(SIDES, around())):
        se, le, de = part(side[0], size_e)
        sn, ln, dn = part(side[1], size_n)
        copy = pltpu.make_async_remote_copy(
            src_ref=x_ref.at[pl.ds(se + 2, le), pl.ds((sn + 2) * 8, ln * 8)],
            dst_ref=ext_ref.at[pl.ds(de, le), pl.ds(dn * 8, ln * 8)],
            send_sem=send.at[i],
            recv_sem=recv.at[i],
            device_id=device,
            device_id_type=MESH,
        )
        copy.start()
        copies.append(copy)
    return copies


def exchange_end(copies, ext_ref):
    for copy in copies:
        copy.wait()
    e, n = lax.axis_index("east"), lax.axis_index("north")
    wide_e, wide_n, lanes = ext_ref.shape

    @pl.when(e == 0)
    def _():
        ext_ref[0:2] = jnp.zeros((2, wide_n, lanes), ext_ref.dtype)

    @pl.when(e == lax.axis_size("east") - 1)
    def _():
        ext_ref[wide_e - 2 : wide_e] = jnp.zeros((2, wide_n, lanes), ext_ref.dtype)

    @pl.when(n == 0)
    def _():
        ext_ref[:, 0:16] = jnp.zeros((wide_e, 16, lanes), ext_ref.dtype)

    @pl.when(n == lax.axis_size("north") - 1)
    def _():
        ext_ref[:, wide_n - 16 : wide_n] = jnp.zeros((wide_e, 16, lanes), ext_ref.dtype)


def build(src_ref, first, planes, start, count, out_ref):
    wide = src_ref.shape[1] // 8
    up = lax.broadcasted_iota(jnp.int32, (wide, 8, 128), 1)

    def body(pair, carry):
        for half in range(2):
            i = pair * 2 + half
            x = src_ref[first + i].astype(F32).reshape(wide, 8, 128)
            below = jnp.where(up == 0, 0.0, pltpu.roll(x, 1, 1))
            above = jnp.where(up == 7, 0.0, pltpu.roll(x, 7, 1))
            rows = pl.ds(pl.multiple_of(i * (count * 8), 16), count * 8)
            for dn in range(3):
                for du, piece in enumerate((below, x, above)):
                    block = (dn * 3 + du) * 128
                    y = piece[start + dn : start + dn + count].reshape(count * 8, 128)
                    out_ref[rows, block : block + 128] = y.astype(BF)
        return carry

    lax.fori_loop(0, planes // 2, body, 0)


def lay_forward(w_ref, out_ref):
    out_ref[...] = jnp.zeros_like(out_ref)
    size = w_ref.shape[1]
    for k in range(27):
        out_ref[k // 9, 0:size, (k % 9) * 128 : (k % 9) * 128 + size] = w_ref[k]


def lay_backward(w_ref, out_ref):
    out_ref[...] = jnp.zeros_like(out_ref)
    size = w_ref.shape[1]
    for k in range(27):
        out_ref[k // 9, (k % 9) * 128 : (k % 9) * 128 + size, 0:size] = w_ref[26 - k]


def product(x, w, transposed):
    if transposed:
        return lax.dot_general(x, w, NT, preferred_element_type=F32)
    return jnp.dot(x, w, preferred_element_type=F32)


def convolve(x_ref, plane, rows, w_ref, acc_ref, transposed):
    total = product(x_ref[0:rows], w_ref[0], transposed)
    for i in (1, 2):
        total = total + product(x_ref[i * plane : i * plane + rows], w_ref[i], transposed)
    acc_ref[0:rows] = total


def build_halo(ext_ref, out_ref):
    planes, rows = ext_ref.shape[0], ext_ref.shape[1] - 16
    inner = planes - 4
    build(ext_ref, 0, 2, 0, rows // 8, out_ref.at[0 : 2 * rows])
    build(ext_ref, planes - 2, 2, 0, rows // 8, out_ref.at[2 * rows + 32 * inner :])
    wide = ext_ref.shape[1] // 8
    up = lax.broadcasted_iota(jnp.int32, (4, 8, 128), 1)
    zero = jnp.zeros((2, 8, 128), F32)

    def body(i, carry):
        x = ext_ref[i + 2].astype(F32).reshape(wide, 8, 128)
        x = jnp.concatenate([x[0:2], x[wide - 2 :]], axis=0)
        below = jnp.where(up == 0, 0.0, pltpu.roll(x, 1, 1))
        above = jnp.where(up == 7, 0.0, pltpu.roll(x, 7, 1))
        at = pl.ds(pl.multiple_of(2 * rows + i * 32, 16), 32)
        for dn in range(3):
            for du, piece in enumerate((below, x, above)):
                block = (dn * 3 + du) * 128
                low = jnp.concatenate([piece[0:2], zero], axis=0)[dn : dn + 2]
                high = jnp.concatenate([zero, piece[2:4]], axis=0)[dn : dn + 2]
                y = jnp.concatenate([low, high], axis=0).reshape(32, 128)
                out_ref[at, block : block + 128] = y.astype(BF)
        return carry

    lax.fori_loop(0, inner, body, 0)


def convolve_halo(x_ref, plane, inner, w_ref, acc_ref, transposed):
    count = 2 * plane + 32 * inner
    last = inner + 1
    for i in range(3):
        y = product(x_ref[i * plane : i * plane + count], w_ref[i], transposed)
        before = (2 - i) * plane
        if before:
            acc_ref[0:before] += y[0:before]
        if i:
            start = (last + 1 - i) * plane
            acc_ref[start : start + i * plane] += y[count - i * plane :]
        for e in range(inner):
            at = (e + 2 - i) * plane
            part = before + e * 32
            acc_ref[at : at + 16] += y[part : part + 16]
            acc_ref[at + plane - 16 : at + plane] += y[part + 16 : part + 32]


def weight_grad(g_ref, x_ref, plane, out_ref, begin=0, end=3):
    size = out_ref.shape[1]

    def body(i, carry):
        x = x_ref[pl.ds(pl.multiple_of(i * plane, 16), g_ref.shape[1])]
        y = jnp.dot(g_ref[...], x, preferred_element_type=F32)
        for b in range(9):
            out_ref[i * 9 + b] = y[0:size, b * 128 : (b + 1) * 128]
        return carry

    lax.fori_loop(0, 3, body, 0)


class Place:
    def __init__(self):
        e, n = lax.axis_index("east"), lax.axis_index("north")
        self.core = lax.rem(e, 2)
        self.z = lax.div(e, 4)
        self.zs = lax.axis_size("east") // 4
        self.xs = lax.axis_size("north") // 2
        self.x = lax.div(n, 2)
        self.y = lax.rem(lax.div(e, 2), 2) * 2 + lax.rem(n, 2)

    def device(self, core=None, x=None, y=None, z=None):
        core = self.core if core is None else core
        x = self.x if x is None else x
        y = self.y if y is None else y
        z = self.z if z is None else z
        return (z * 4 + lax.div(y, 2) * 2 + core, x * 2 + lax.rem(y, 2))

    def partner(self):
        return self.device(core=1 - self.core)

    def plane(self):
        steps = [(a, b) for a in range(self.xs) for b in range(4) if (a, b) != (0, 0)]
        steps.sort(key=lambda s: (min(s[0], self.xs - s[0]) + min(s[1], 4 - s[1]), s))
        found = []
        for a, b in steps:
            x, y = lax.rem(self.x + a, self.xs), lax.rem(self.y + b, 4)
            back = steps.index(((self.xs - a) % self.xs, (4 - b) % 4))
            found.append((x * 4 + y, self.device(x=x, y=y), back))
        return found

    def column(self):
        found = []
        for step in range(1, self.zs):
            found.append(self.device(z=lax.rem(self.z + step, self.zs)))
        return found

    def peers(self):
        return [self.partner()] + [device for _, device, _ in self.plane()] + self.column()


def all_reduce(place, src, full, away, got_core, held, got, slots, send, recv):
    half = src.shape[0] // 2
    plane = place.plane()
    piece = half // (len(plane) + 1)
    started = []

    def go(a, b, device):
        i = len(started)
        copy = pltpu.make_async_remote_copy(
            src_ref=a, dst_ref=b, send_sem=send.at[i], recv_sem=recv.at[i],
            device_id=device, device_id_type=MESH,
        )
        copy.start()
        started.append(copy)
        return copy

    def at(start, size):
        return pl.ds(pl.multiple_of(start, 32), size)

    mine = place.core * half
    theirs = (1 - place.core) * half

    def cast(i, carry):
        away[at(i * 256, 256)] = src[at(theirs + i * 256, 256)].astype(BF)
        return carry

    lax.fori_loop(0, half // 256, cast, 0)
    copies = [go(away, got_core, place.partner())]
    yield

    for copy in copies:
        copy.wait_recv()

    def pair(i, carry):
        total = src[at(mine + i * 256, 256)] + got_core[at(i * 256, 256)].astype(F32)
        held[at(i * 256, 256)] = total.astype(BF)
        return carry

    lax.fori_loop(0, half // 256, pair, 0)
    copies = []
    for i, (there, device, _) in enumerate(plane):
        copies.append(go(held.at[at(there * piece, piece)], got.at[i], device))
    yield

    own = (place.x * 4 + place.y) * piece
    total = src[at(mine + own, piece)] + got_core[at(own, piece)].astype(F32)
    for i, copy in enumerate(copies):
        copy.wait_recv()
        total = total + got[i].astype(F32)
    slots[place.z] = total.astype(BF)
    copies = []
    for device in place.column():
        copies.append(go(slots.at[place.z], slots.at[place.z], device))
    yield

    for copy in copies:
        copy.wait_recv()
    total = slots[0].astype(F32)
    for z in range(1, place.zs):
        total = total + slots[z].astype(F32)
    rows = at(mine + own, piece)
    full[rows] = total.astype(BF)
    copies = []
    for _, device, _ in plane:
        copies.append(go(full.at[rows], full.at[rows], device))
    last = [go(full.at[rows], full.at[rows], place.partner())]
    yield

    for copy, (_, _, back) in zip(copies, plane):
        copy.wait_recv()
        rows = at(mine + plane[back][0] * piece, piece)
        last.append(go(full.at[rows], full.at[rows], place.partner()))
    copies = last
    yield

    for copy in copies:
        copy.wait_recv()
    for copy in started:
        copy.wait_send()
    yield


REDUCE_COPIES = 56


def reduce_scratch(rows, places, zs):
    half = rows // 2
    piece = half // places
    return [
        VM((rows, 128), BF),
        VM((half, 128), BF),
        VM((half, 128), BF),
        VM((half, 128), BF),
        VM((places - 1, piece, 128), BF),
        VM((zs, piece, 128), BF),
        pltpu.SemaphoreType.DMA((REDUCE_COPIES,)),
        pltpu.SemaphoreType.DMA((REDUCE_COPIES,)),
    ]


PACKED = 2048


def pack(grad_ref, out_ref, begin=0, end=6):
    size = grad_ref.shape[1]
    lane = lax.broadcasted_iota(jnp.int32, (size, 128), 1)

    def body(g, carry):
        spare = grad_ref[g * 4 + 3]
        for j in range(3):
            moved = pltpu.roll(spare, 96 - 32 * j, 1)
            rows = pl.ds(pl.multiple_of((g * 3 + j) * size, 32), size)
            out_ref[rows] = jnp.where(lane < 96, grad_ref[g * 4 + j], moved)
        return carry

    lax.fori_loop(begin, end, body, 0)
    if end < 6:
        return
    for j in range(3):
        out_ref[(18 + j) * size : (19 + j) * size] = grad_ref[24 + j]
    out_ref[21 * size :] = jnp.zeros((out_ref.shape[0] - 21 * size, 128), F32)


def unpack(full_ref, out_ref, scale, out_hbm, sems):
    size = out_ref.shape[1]
    lane = lax.broadcasted_iota(jnp.int32, (size, 128), 1)
    copies = []

    def take(block):
        return full_ref[block * size : (block + 1) * size].astype(F32) * scale

    def put(start, count):
        part = pl.ds(start, count)
        copy = pltpu.make_async_copy(out_ref.at[part], out_hbm.at[part], sems.at[len(copies)])
        copy.start()
        copies.append(copy)

    for g in range(6):
        spare = []
        for j in range(3):
            value = take(g * 3 + j)
            out_ref[g * 4 + j] = value[:, 0:size]
            spare.append(pltpu.roll(value, 32 + 32 * j, 1))
        value = jnp.where(lane < 32, spare[0], jnp.where(lane < 64, spare[1], spare[2]))
        out_ref[g * 4 + 3] = value[:, 0:size]
        put(g * 4, 4)
    for j in range(3):
        out_ref[24 + j] = take(18 + j)[:, 0:size]
    put(24, 3)
    return copies


def slope_of(value, sig):
    return sig * (1.0 + value * (1.0 - sig))


def lay_teacher(teacher_ref, flat_ref, out_ref):
    classes, east, up, north = teacher_ref.shape
    flat_ref[...] = teacher_ref[...].astype(F32).reshape(flat_ref.shape)
    rows = classes * east
    parts = [flat_ref[pl.ds(u, rows, stride=up), :] for u in range(up)]
    wide = jnp.concatenate(parts, axis=1).astype(BF)
    wide = jnp.concatenate([wide, jnp.zeros((128 - rows, 128), BF)], axis=0)
    turned = lax.dot_general(reorder(up, north), wide, NT, preferred_element_type=F32)
    out_ref[...] = turned.astype(BF)


def reorder(up, north):
    row = lax.broadcasted_iota(jnp.int32, (up * north, up * north), 0)
    col = lax.broadcasted_iota(jnp.int32, (up * north, up * north), 1)
    return jnp.where(col == (row % up) * north + row // up, 1.0, 0.0).astype(BF)


def fill(features_ref, brick_ref, occupancy_ref, ext_ref, own_ref):
    east, up, north = occupancy_ref.shape
    channels = features_ref.shape[2]
    bricks = brick_ref.shape[0]
    brick = lax.broadcasted_iota(jnp.int32, (east, north), 1) // (north // bricks)
    flags = jnp.zeros((east, north), jnp.int32)
    for b in range(bricks):
        flags = jnp.where(brick == b, brick_ref[b], flags)
    parts = [(occupancy_ref[:, u, :] * flags).astype(F32) for u in range(up)]
    wide = jnp.concatenate(parts, axis=1).astype(BF)
    mask = lax.dot_general(reorder(up, north), wide, NT, preferred_element_type=F32)
    rows = up * north
    lane = lax.broadcasted_iota(jnp.int32, (rows, 128 - channels), 1)
    for e in range(east):
        column = mask[:, e : e + 1]
        x = features_ref[e].astype(F32)
        kept = jnp.where(jnp.broadcast_to(column, x.shape) > 0, x, 0.0)
        spare = jnp.where(lane == 0, jnp.broadcast_to(column, lane.shape), 0.0)
        both = jnp.concatenate([kept, spare], axis=1)
        ext_ref[e + 2, 16 : 16 + rows] = both.astype(BF)
        own_ref[e + 2, 16 : 16 + rows] = both.astype(BF)


def main_kernel(
    features_hbm, brick_ref, occupancy_hbm, w1_hbm, w2_hbm, head_ref, teacher_hbm,
    out_hbm, full1_hbm, full2_hbm,
    ext0_ref, own_ref, halo_cols, ext2_ref, w1_ref, w2_ref, wf1, wf2, wb1, wb2, wide_head, flat_teacher, turned,
    cols0, cols1, cols2, acc, a1_ref, slope_ref, g1_ref, gt_ref, part_ref,
    packed1_ref, packed2_ref, out_ref, features_ref, occupancy_ref, teacher_ref,
    send0, recv0, send2, recv2, local, *rest,
):
    place = Place()
    devices = around() + place.peers()
    barrier = pltpu.get_barrier_semaphore()
    for device in devices:
        pl.semaphore_signal(barrier, inc=1, device_id=device, device_id_type=MESH)
    pairs = (
        (features_hbm, features_ref), (occupancy_hbm, occupancy_ref),
        (w1_hbm, w1_ref), (w2_hbm, w2_ref), (teacher_hbm, teacher_ref),
    )
    loads = [pltpu.make_async_copy(a, b, local.at[3 + i]) for i, (a, b) in enumerate(pairs)]
    for load in loads:
        load.start()
    split = packed1_ref.shape[0] // 2
    two = all_reduce(place, packed2_ref, *rest[:8])
    one_a = all_reduce(place, packed1_ref.at[0:split], *rest[8:16])
    one_b = all_reduce(place, packed1_ref.at[split:], *rest[16:24])
    size_e, rows, channels = features_ref.shape
    classes = head_ref.shape[0]
    north = rows // 8
    wide = rows + 16

    loads[0].wait()
    loads[1].wait()
    fill(features_ref, brick_ref, occupancy_ref, ext0_ref, own_ref)
    pl.semaphore_wait(barrier, len(devices))
    copies = exchange_start(own_ref, ext0_ref, send0, recv0)
    edge = jnp.zeros((size_e + 4, 16, 128), BF)
    own_ref[:, 0:16] = edge
    own_ref[:, 16 + rows : 32 + rows] = edge
    cols1[0 : 2 * wide] = jnp.zeros((2 * wide, cols1.shape[1]), BF)
    cols1[(size_e + 2) * wide :] = jnp.zeros((2 * wide, cols1.shape[1]), BF)
    build(own_ref, 2, size_e, 0, north + 2, cols1.at[2 * wide : (size_e + 2) * wide])
    loads[2].wait()
    lay_forward(w1_ref, wf1)
    convolve(cols1, wide, (size_e + 2) * wide, wf1, acc, True)
    loads[3].wait()
    lay_forward(w2_ref, wf2)
    wide_head[...] = jnp.zeros_like(wide_head)
    wide_head[0:classes, 0:channels] = head_ref[...]
    loads[4].wait()
    lay_teacher(teacher_ref, flat_teacher, turned)
    exchange_end(copies, ext0_ref)
    build_halo(ext0_ref, halo_cols)
    convolve_halo(halo_cols, wide, size_e, wf1, acc, True)

    def first(pair, carry):
        for half in range(2):
            i = pair * 2 + half
            at = pl.ds(pl.multiple_of(i * wide, 16), wide)
            x = ext0_ref[i + 1].astype(F32)[8 : 8 + wide]
            mask = jnp.broadcast_to(x[:, channels : channels + 1], (wide, 128))
            p1 = mask * acc[at]
            sig = jax.nn.sigmoid(p1)
            a1_ref[i] = (p1 * sig).astype(BF)
            slope_ref[at] = mask * slope_of(p1, sig)
        return carry

    lax.fori_loop(0, (size_e + 2) // 2, first, 0)
    build(a1_ref, 0, size_e + 2, 0, north, cols2)
    convolve(cols2, rows, size_e * rows, wf2, acc, True)
    head = wide_head[...]
    row = lax.broadcasted_iota(jnp.int32, (128, 128), 0)
    col = lax.broadcasted_iota(jnp.int32, (128, 128), 1)

    group = size_e

    def second(i, carry):
        planes = pl.ds(i * group + 2, group)
        at = pl.ds(pl.multiple_of(i * (group * rows), 128), group * rows)
        x = ext0_ref[planes, 16 : 16 + rows].astype(F32).reshape(group * rows, 128)
        mask = jnp.broadcast_to(x[:, channels : channels + 1], (group * rows, 128))
        p2 = mask * acc[at]
        sig = jax.nn.sigmoid(p2)
        a2 = (p2 * sig).astype(BF)
        logits = lax.dot_general(a2, head, NT, preferred_element_type=F32)
        teacher = []
        for b in range(group):
            pick = (row == col * size_e + (i * group + b)) & (col < classes)
            pick = jnp.where(pick, 1.0, 0.0).astype(BF)
            teacher.append(jnp.dot(turned[...], pick, preferred_element_type=F32))
        g = mask * (logits - jnp.concatenate(teacher, axis=0))
        high = g.astype(BF)
        left = g - high.astype(F32)
        mid = left.astype(BF)
        low = (left - mid.astype(F32)).astype(BF)
        back = jnp.dot(low, head, preferred_element_type=F32)
        back = back + jnp.dot(mid, head, preferred_element_type=F32)
        back = back + jnp.dot(high, head, preferred_element_type=F32)
        g2 = (mask * back * slope_of(p2, sig)).astype(BF)
        ext2_ref[planes, 16 : 16 + rows] = g2.reshape(group, rows, 128)
        gt_ref[:, at] = g2.astype(F32).T.astype(BF)
        return carry

    lax.fori_loop(0, size_e // group, second, 0)
    copies = exchange_start(ext2_ref, ext2_ref, send2, recv2)
    weight_grad(gt_ref, cols2, rows, part_ref)
    pack(part_ref, packed2_ref)
    next(two)
    lay_backward(w2_ref, wb2)
    lay_backward(w1_ref, wb1)
    build(ext0_ref, 1, size_e + 2, 1, north, cols0)
    next(two)
    exchange_end(copies, ext2_ref)
    build(ext2_ref, 0, size_e + 4, 0, north + 2, cols1)
    convolve(cols1, wide, (size_e + 2) * wide, wb2, acc, False)
    next(two)

    for i in range(size_e + 2):
        g1 = (acc[i * wide : (i + 1) * wide] * slope_ref[i * wide : (i + 1) * wide]).astype(BF)
        g1_ref[i] = g1
        if 0 < i <= size_e:
            gt_ref[:, (i - 1) * rows : i * rows] = g1.astype(F32)[8 : 8 + rows].T.astype(BF)
    weight_grad(gt_ref, cols0, rows, part_ref, 0, 2)
    pack(part_ref, packed1_ref, 0, 4)
    next(one_a)
    weight_grad(gt_ref, cols0, rows, part_ref, 2, 3)
    pack(part_ref, packed1_ref, 4, 6)
    next(one_b)
    next(one_a)
    next(one_b)
    build(g1_ref, 0, size_e + 2, 0, north, cols2)
    next(two)
    convolve(cols2, rows, size_e * rows, wb1, acc, False)

    def last(i, carry):
        at = pl.ds(pl.multiple_of(i * rows, 16), rows)
        x = ext0_ref[i + 2, 16 : 16 + rows].astype(F32)
        mask = jnp.broadcast_to(x[:, channels : channels + 1], (rows, 128))
        out_ref[i] = (mask * acc[at])[:, 0:channels].astype(BF)
        return carry

    lax.fori_loop(0, size_e, last, 0)
    saved = pltpu.make_async_copy(out_ref, out_hbm, local.at[0])
    saved.start()
    next(one_a)
    next(one_b)
    next(two)
    next(one_a)
    next(one_b)
    next(two)
    put2 = pltpu.make_async_copy(rest[0], full2_hbm, local.at[1])
    put2.start()
    next(one_a)
    next(one_b)
    next(one_a)
    put1a = pltpu.make_async_copy(rest[8], full1_hbm.at[0:split], local.at[2])
    put1a.start()
    next(one_b)
    put1b = pltpu.make_async_copy(rest[16], full1_hbm.at[pl.ds(split, split)], local.at[3])
    put1b.start()
    saved.wait()
    put2.wait()
    put1a.wait()
    put1b.wait()


def finish_kernel(
    scale, out_in, full1_in, full2_in, out_hbm, grad1_hbm, grad2_hbm,
    out_ref, full1_ref, full2_ref, grad1_ref, grad2_ref, loads, stores1, stores2,
):
    pairs = ((full2_in, full2_ref), (full1_in, full1_ref), (out_in, out_ref))
    copies = [pltpu.make_async_copy(a, b, loads.at[i]) for i, (a, b) in enumerate(pairs)]
    for copy in copies:
        copy.start()
    copies[0].wait()
    stores = unpack(full2_ref, grad2_ref, scale, grad2_hbm, stores2)
    copies[1].wait()
    stores += unpack(full1_ref, grad1_ref, scale, grad1_hbm, stores1)
    copies[2].wait()
    saved = pltpu.make_async_copy(out_ref, out_hbm, loads.at[3])
    saved.start()
    for copy in stores + [saved]:
        copy.wait()


def per_device(
    features, brick_active, voxel_occupancy, first_weights, second_weights, head, teacher
):
    channels, east, north, upward = features.shape
    classes = head.shape[0]
    rows = north * upward
    shape = jax.ShapeDtypeStruct
    sems = pltpu.SemaphoreType.DMA
    wide = rows + 16
    ext = VM((east + 4, rows + 32, 128), BF)
    field = VM((east + 2, wide, 128), BF)
    weights = VM(first_weights.shape, BF)
    forward, backward = VM((3, 128, 1152), BF), VM((3, 1152, 128), BF)
    narrow_cols = VM(((east + 2) * rows, 1152), BF)
    out = shape((east, rows, channels), BF)
    full = shape((PACKED, 128), BF)
    grad = shape((27, channels, channels), F32)
    vmem, anywhere = pl.BlockSpec(memory_space=VM), pl.BlockSpec(memory_space=pl.ANY)
    packed = VM((PACKED, 128), F32)
    result = pl.pallas_call(
        main_kernel,
        out_shape=(out, full, full),
        in_specs=[anywhere, pl.BlockSpec(memory_space=pltpu.SMEM), anywhere, anywhere, anywhere, vmem, anywhere],
        out_specs=[anywhere] * 3,
        scratch_shapes=[
            ext, ext, VM((4 * wide + 32 * east, 1152), BF), ext, weights, weights, forward, forward, backward, backward,
            VM((128, 128), BF),
            VM((classes * east * upward, north), F32),
            VM((128, 128), BF),
            narrow_cols, VM(((east + 4) * wide, 1152), BF), narrow_cols,
            VM(((east + 2) * wide, 128), F32),
            field,
            VM(((east + 2) * wide, 128), F32),
            field,
            VM((128, east * rows), BF),
            VM((27, channels, 128), F32),
            packed, packed,
            VM((east, rows, channels), BF),
            VM((east, rows, channels), BF),
            VM((east, upward, north), jnp.int32),
            VM(head.shape[:1] + (east, upward, north), BF),
            sems((8,)), sems((8,)), sems((8,)), sems((8,)), sems((8,)),
        ]
        + [
            item
            for size in (PACKED, PACKED // 2, PACKED // 2)
            for item in reduce_scratch(size, lax.axis_size("north") * 2, lax.axis_size("east") // 4)
        ],
        compiler_params=pltpu.CompilerParams(
            collective_id=1, has_side_effects=True, vmem_limit_bytes=60 << 20
        ),
    )(
        features.transpose(1, 2, 3, 0).reshape(east, rows, channels),
        brick_active.reshape(-1),
        voxel_occupancy.transpose(0, 2, 1),
        first_weights,
        second_weights,
        head,
        teacher.transpose(0, 1, 3, 2),
    )
    total_voxels = lax.axis_size("east") * lax.axis_size("north") * east * north * upward
    scale = 1.0 / math.sqrt(total_voxels)
    grad_features, grad_first, grad_second = pl.pallas_call(
        functools.partial(finish_kernel, scale),
        out_shape=(out, grad, grad),
        in_specs=[anywhere] * 3,
        out_specs=[anywhere] * 3,
        scratch_shapes=[VM(a.shape, a.dtype) for a in (out, full, full, grad, grad)]
        + [sems((4,)), sems((7,)), sems((7,))],
        compiler_params=pltpu.CompilerParams(vmem_limit_bytes=60 << 20),
    )(*result)
    grad_features = grad_features.reshape(east, north, upward, channels).transpose(3, 0, 1, 2)
    return (grad_features, grad_first, grad_second)


def solution(mesh):
    in_specs = (
        P(None, "east", "north", None),
        P("east", "north", None),
        P("east", "north", None),
        P(),
        P(),
        P(),
        P(None, "east", "north", None),
    )
    out_specs = (P(None, "east", "north", None), P(), P())
    return jax.shard_map(
        per_device, mesh=mesh, in_specs=in_specs, out_specs=out_specs, check_vma=False
    )
```

```python
import functools
import math

import jax
import jax.numpy as jnp
from jax import lax
from jax.experimental import pallas as pl
from jax.experimental.pallas import tpu as pltpu
from jax.sharding import PartitionSpec as P

MESH = pl.DeviceIdType.MESH
VM = pltpu.VMEM
F32 = jnp.float32
BF = jnp.bfloat16
SIDES = ((-1, -1), (-1, 1), (1, -1), (1, 1), (-1, 0), (1, 0), (0, -1), (0, 1))
NT = (((1,), (1,)), ((), ()))


def part(side, size):
    if side > 0:
        return size - 2, 2, 0
    if side < 0:
        return 0, 2, size + 2
    return 0, size, 2


def around():
    east, north = lax.axis_size("east"), lax.axis_size("north")
    e, n = lax.axis_index("east"), lax.axis_index("north")
    return [(lax.rem(e + a + east, east), lax.rem(n + b + north, north)) for a, b in SIDES]


def exchange_start(x_ref, ext_ref, send, recv):
    size_e, size_n = ext_ref.shape[0] - 4, ext_ref.shape[1] // 8 - 4
    copies = []
    for i, (side, device) in enumerate(zip(SIDES, around())):
        se, le, de = part(side[0], size_e)
        sn, ln, dn = part(side[1], size_n)
        copy = pltpu.make_async_remote_copy(
            src_ref=x_ref.at[pl.ds(se + 2, le), pl.ds((sn + 2) * 8, ln * 8)],
            dst_ref=ext_ref.at[pl.ds(de, le), pl.ds(dn * 8, ln * 8)],
            send_sem=send.at[i],
            recv_sem=recv.at[i],
            device_id=device,
            device_id_type=MESH,
        )
        copy.start()
        copies.append(copy)
    return copies


def exchange_end(copies, ext_ref):
    for copy in copies:
        copy.wait()
    e, n = lax.axis_index("east"), lax.axis_index("north")
    wide_e, wide_n, lanes = ext_ref.shape

    @pl.when(e == 0)
    def _():
        ext_ref[0:2] = jnp.zeros((2, wide_n, lanes), ext_ref.dtype)

    @pl.when(e == lax.axis_size("east") - 1)
    def _():
        ext_ref[wide_e - 2 : wide_e] = jnp.zeros((2, wide_n, lanes), ext_ref.dtype)

    @pl.when(n == 0)
    def _():
        ext_ref[:, 0:16] = jnp.zeros((wide_e, 16, lanes), ext_ref.dtype)

    @pl.when(n == lax.axis_size("north") - 1)
    def _():
        ext_ref[:, wide_n - 16 : wide_n] = jnp.zeros((wide_e, 16, lanes), ext_ref.dtype)


def build(src_ref, first, planes, start, count, out_ref):
    wide = src_ref.shape[1] // 8
    up = lax.broadcasted_iota(jnp.int32, (wide, 8, 128), 1)

    def body(pair, carry):
        for half in range(2):
            i = pair * 2 + half
            x = src_ref[first + i].astype(F32).reshape(wide, 8, 128)
            below = jnp.where(up == 0, 0.0, pltpu.roll(x, 1, 1))
            above = jnp.where(up == 7, 0.0, pltpu.roll(x, 7, 1))
            rows = pl.ds(pl.multiple_of(i * (count * 8), 16), count * 8)
            for dn in range(3):
                for du, piece in enumerate((below, x, above)):
                    block = (dn * 3 + du) * 128
                    y = piece[start + dn : start + dn + count].reshape(count * 8, 128)
                    out_ref[rows, block : block + 128] = y.astype(BF)
        return carry

    lax.fori_loop(0, planes // 2, body, 0)


def lay_forward(w_ref, out_ref):
    out_ref[...] = jnp.zeros_like(out_ref)
    size = w_ref.shape[1]
    for k in range(27):
        out_ref[k // 9, 0:size, (k % 9) * 128 : (k % 9) * 128 + size] = w_ref[k]


def lay_backward(w_ref, out_ref):
    out_ref[...] = jnp.zeros_like(out_ref)
    size = w_ref.shape[1]
    for k in range(27):
        out_ref[k // 9, (k % 9) * 128 : (k % 9) * 128 + size, 0:size] = w_ref[26 - k]


def product(x, w, transposed):
    if transposed:
        return lax.dot_general(x, w, NT, preferred_element_type=F32)
    return jnp.dot(x, w, preferred_element_type=F32)


def convolve(x_ref, plane, rows, w_ref, acc_ref, transposed):
    total = product(x_ref[0:rows], w_ref[0], transposed)
    for i in (1, 2):
        total = total + product(x_ref[i * plane : i * plane + rows], w_ref[i], transposed)
    acc_ref[0:rows] = total


def build_halo(ext_ref, out_ref):
    planes, rows = ext_ref.shape[0], ext_ref.shape[1] - 16
    inner = planes - 4
    build(ext_ref, 0, 2, 0, rows // 8, out_ref.at[0 : 2 * rows])
    build(ext_ref, planes - 2, 2, 0, rows // 8, out_ref.at[2 * rows + 32 * inner :])
    wide = ext_ref.shape[1] // 8
    up = lax.broadcasted_iota(jnp.int32, (4, 8, 128), 1)
    zero = jnp.zeros((2, 8, 128), F32)

    def body(i, carry):
        x = ext_ref[i + 2].astype(F32).reshape(wide, 8, 128)
        x = jnp.concatenate([x[0:2], x[wide - 2 :]], axis=0)
        below = jnp.where(up == 0, 0.0, pltpu.roll(x, 1, 1))
        above = jnp.where(up == 7, 0.0, pltpu.roll(x, 7, 1))
        at = pl.ds(pl.multiple_of(2 * rows + i * 32, 16), 32)
        for dn in range(3):
            for du, piece in enumerate((below, x, above)):
                block = (dn * 3 + du) * 128
                low = jnp.concatenate([piece[0:2], zero], axis=0)[dn : dn + 2]
                high = jnp.concatenate([zero, piece[2:4]], axis=0)[dn : dn + 2]
                y = jnp.concatenate([low, high], axis=0).reshape(32, 128)
                out_ref[at, block : block + 128] = y.astype(BF)
        return carry

    lax.fori_loop(0, inner, body, 0)


def convolve_halo(x_ref, plane, inner, w_ref, acc_ref, transposed):
    count = 2 * plane + 32 * inner
    last = inner + 1
    for i in range(3):
        y = product(x_ref[i * plane : i * plane + count], w_ref[i], transposed)
        before = (2 - i) * plane
        if before:
            acc_ref[0:before] += y[0:before]
        if i:
            start = (last + 1 - i) * plane
            acc_ref[start : start + i * plane] += y[count - i * plane :]
        for e in range(inner):
            at = (e + 2 - i) * plane
            part = before + e * 32
            acc_ref[at : at + 16] += y[part : part + 16]
            acc_ref[at + plane - 16 : at + plane] += y[part + 16 : part + 32]


def weight_grad(g_ref, x_ref, plane, out_ref, begin=0, end=3):
    size = out_ref.shape[1]

    def body(i, carry):
        x = x_ref[pl.ds(pl.multiple_of(i * plane, 16), g_ref.shape[1])]
        y = jnp.dot(g_ref[...], x, preferred_element_type=F32)
        for b in range(9):
            out_ref[i * 9 + b] = y[0:size, b * 128 : (b + 1) * 128]
        return carry

    lax.fori_loop(0, 3, body, 0)


class Place:
    def __init__(self):
        e, n = lax.axis_index("east"), lax.axis_index("north")
        self.core = lax.rem(e, 2)
        self.z = lax.div(e, 4)
        self.zs = lax.axis_size("east") // 4
        self.xs = lax.axis_size("north") // 2
        self.x = lax.div(n, 2)
        self.y = lax.rem(lax.div(e, 2), 2) * 2 + lax.rem(n, 2)

    def device(self, core=None, x=None, y=None, z=None):
        core = self.core if core is None else core
        x = self.x if x is None else x
        y = self.y if y is None else y
        z = self.z if z is None else z
        return (z * 4 + lax.div(y, 2) * 2 + core, x * 2 + lax.rem(y, 2))

    def partner(self):
        return self.device(core=1 - self.core)

    def plane(self):
        steps = [(a, b) for a in range(self.xs) for b in range(4) if (a, b) != (0, 0)]
        steps.sort(key=lambda s: (min(s[0], self.xs - s[0]) + min(s[1], 4 - s[1]), s))
        found = []
        for a, b in steps:
            x, y = lax.rem(self.x + a, self.xs), lax.rem(self.y + b, 4)
            back = steps.index(((self.xs - a) % self.xs, (4 - b) % 4))
            found.append((x * 4 + y, self.device(x=x, y=y), back))
        return found

    def column(self):
        found = []
        for step in range(1, self.zs):
            found.append(self.device(z=lax.rem(self.z + step, self.zs)))
        return found

    def peers(self):
        return [self.partner()] + [device for _, device, _ in self.plane()] + self.column()


def all_reduce(place, src, full, away, got_core, held, got, slots, send, recv):
    half = src.shape[0] // 2
    plane = place.plane()
    piece = half // (len(plane) + 1)
    started = []

    def go(a, b, device):
        i = len(started)
        copy = pltpu.make_async_remote_copy(
            src_ref=a, dst_ref=b, send_sem=send.at[i], recv_sem=recv.at[i],
            device_id=device, device_id_type=MESH,
        )
        copy.start()
        started.append(copy)
        return copy

    def at(start, size):
        return pl.ds(pl.multiple_of(start, 32), size)

    mine = place.core * half
    theirs = (1 - place.core) * half

    def cast(i, carry):
        away[at(i * 256, 256)] = src[at(theirs + i * 256, 256)].astype(BF)
        return carry

    lax.fori_loop(0, half // 256, cast, 0)
    copies = [go(away, got_core, place.partner())]
    yield

    for copy in copies:
        copy.wait_recv()

    def pair(i, carry):
        total = src[at(mine + i * 256, 256)] + got_core[at(i * 256, 256)].astype(F32)
        held[at(i * 256, 256)] = total.astype(BF)
        return carry

    lax.fori_loop(0, half // 256, pair, 0)
    copies = []
    for i, (there, device, _) in enumerate(plane):
        copies.append(go(held.at[at(there * piece, piece)], got.at[i], device))
    yield

    own = (place.x * 4 + place.y) * piece
    total = src[at(mine + own, piece)] + got_core[at(own, piece)].astype(F32)
    for i, copy in enumerate(copies):
        copy.wait_recv()
        total = total + got[i].astype(F32)
    slots[place.z] = total.astype(BF)
    copies = []
    for device in place.column():
        copies.append(go(slots.at[place.z], slots.at[place.z], device))
    yield

    for copy in copies:
        copy.wait_recv()
    total = slots[0].astype(F32)
    for z in range(1, place.zs):
        total = total + slots[z].astype(F32)
    rows = at(mine + own, piece)
    full[rows] = total.astype(BF)
    copies = []
    for _, device, _ in plane:
        copies.append(go(full.at[rows], full.at[rows], device))
    last = [go(full.at[rows], full.at[rows], place.partner())]
    yield

    for copy, (_, _, back) in zip(copies, plane):
        copy.wait_recv()
        rows = at(mine + plane[back][0] * piece, piece)
        last.append(go(full.at[rows], full.at[rows], place.partner()))
    copies = last
    yield

    for copy in copies:
        copy.wait_recv()
    for copy in started:
        copy.wait_send()
    yield


REDUCE_COPIES = 56


def reduce_scratch(rows, places, zs):
    half = rows // 2
    piece = half // places
    return [
        VM((rows, 128), BF),
        VM((half, 128), BF),
        VM((half, 128), BF),
        VM((half, 128), BF),
        VM((places - 1, piece, 128), BF),
        VM((zs, piece, 128), BF),
        pltpu.SemaphoreType.DMA((REDUCE_COPIES,)),
        pltpu.SemaphoreType.DMA((REDUCE_COPIES,)),
    ]


PACKED = 2048


def pack(grad_ref, out_ref, begin=0, end=6):
    size = grad_ref.shape[1]
    lane = lax.broadcasted_iota(jnp.int32, (size, 128), 1)

    def body(g, carry):
        spare = grad_ref[g * 4 + 3]
        for j in range(3):
            moved = pltpu.roll(spare, 96 - 32 * j, 1)
            rows = pl.ds(pl.multiple_of((g * 3 + j) * size, 32), size)
            out_ref[rows] = jnp.where(lane < 96, grad_ref[g * 4 + j], moved)
        return carry

    lax.fori_loop(begin, end, body, 0)
    if end < 6:
        return
    for j in range(3):
        out_ref[(18 + j) * size : (19 + j) * size] = grad_ref[24 + j]
    out_ref[21 * size :] = jnp.zeros((out_ref.shape[0] - 21 * size, 128), F32)


def unpack(full_ref, out_ref, scale, out_hbm, sems):
    size = out_ref.shape[1]
    lane = lax.broadcasted_iota(jnp.int32, (size, 128), 1)
    copies = []

    def take(block):
        return full_ref[block * size : (block + 1) * size].astype(F32) * scale

    def put(start, count):
        part = pl.ds(start, count)
        copy = pltpu.make_async_copy(out_ref.at[part], out_hbm.at[part], sems.at[len(copies)])
        copy.start()
        copies.append(copy)

    for g in range(6):
        spare = []
        for j in range(3):
            value = take(g * 3 + j)
            out_ref[g * 4 + j] = value[:, 0:size]
            spare.append(pltpu.roll(value, 32 + 32 * j, 1))
        value = jnp.where(lane < 32, spare[0], jnp.where(lane < 64, spare[1], spare[2]))
        out_ref[g * 4 + 3] = value[:, 0:size]
        put(g * 4, 4)
    for j in range(3):
        out_ref[24 + j] = take(18 + j)[:, 0:size]
    put(24, 3)
    return copies


def slope_of(value, sig):
    return sig * (1.0 + value * (1.0 - sig))


def lay_teacher(teacher_ref, flat_ref, out_ref):
    classes, east, up, north = teacher_ref.shape
    flat_ref[...] = teacher_ref[...].astype(F32).reshape(flat_ref.shape)
    rows = classes * east
    parts = [flat_ref[pl.ds(u, rows, stride=up), :] for u in range(up)]
    wide = jnp.concatenate(parts, axis=1).astype(BF)
    wide = jnp.concatenate([wide, jnp.zeros((128 - rows, 128), BF)], axis=0)
    turned = lax.dot_general(reorder(up, north), wide, NT, preferred_element_type=F32)
    out_ref[...] = turned.astype(BF)


def reorder(up, north):
    row = lax.broadcasted_iota(jnp.int32, (up * north, up * north), 0)
    col = lax.broadcasted_iota(jnp.int32, (up * north, up * north), 1)
    return jnp.where(col == (row % up) * north + row // up, 1.0, 0.0).astype(BF)


def fill(features_ref, brick_ref, occupancy_ref, ext_ref, own_ref):
    east, up, north = occupancy_ref.shape
    channels = features_ref.shape[2]
    bricks = brick_ref.shape[0]
    brick = lax.broadcasted_iota(jnp.int32, (east, north), 1) // (north // bricks)
    flags = jnp.zeros((east, north), jnp.int32)
    for b in range(bricks):
        flags = jnp.where(brick == b, brick_ref[b], flags)
    parts = [(occupancy_ref[:, u, :] * flags).astype(F32) for u in range(up)]
    wide = jnp.concatenate(parts, axis=1).astype(BF)
    mask = lax.dot_general(reorder(up, north), wide, NT, preferred_element_type=F32)
    rows = up * north
    lane = lax.broadcasted_iota(jnp.int32, (rows, 128 - channels), 1)
    for e in range(east):
        column = mask[:, e : e + 1]
        x = features_ref[e].astype(F32)
        kept = jnp.where(jnp.broadcast_to(column, x.shape) > 0, x, 0.0)
        spare = jnp.where(lane == 0, jnp.broadcast_to(column, lane.shape), 0.0)
        both = jnp.concatenate([kept, spare], axis=1)
        ext_ref[e + 2, 16 : 16 + rows] = both.astype(BF)
        own_ref[e + 2, 16 : 16 + rows] = both.astype(BF)


def main_kernel(
    features_hbm, brick_ref, occupancy_hbm, w1_hbm, w2_hbm, head_ref, teacher_hbm,
    out_hbm, full1_hbm, full2_hbm,
    ext0_ref, own_ref, halo_cols, ext2_ref, w1_ref, w2_ref, wf1, wf2, wb1, wb2, wide_head, flat_teacher, turned,
    cols0, cols1, cols2, acc, a1_ref, slope_ref, g1_ref, gt_ref, part_ref,
    packed1_ref, packed2_ref, out_ref, features_ref, occupancy_ref, teacher_ref,
    send0, recv0, send2, recv2, local, *rest,
):
    place = Place()
    devices = around() + place.peers()
    barrier = pltpu.get_barrier_semaphore()
    for device in devices:
        pl.semaphore_signal(barrier, inc=1, device_id=device, device_id_type=MESH)
    pairs = (
        (features_hbm, features_ref), (occupancy_hbm, occupancy_ref),
        (w1_hbm, w1_ref), (w2_hbm, w2_ref), (teacher_hbm, teacher_ref),
    )
    loads = [pltpu.make_async_copy(a, b, local.at[3 + i]) for i, (a, b) in enumerate(pairs)]
    for load in loads:
        load.start()
    split = packed1_ref.shape[0] // 2
    two = all_reduce(place, packed2_ref, *rest[:8])
    one_a = all_reduce(place, packed1_ref.at[0:split], *rest[8:16])
    one_b = all_reduce(place, packed1_ref.at[split:], *rest[16:24])
    size_e, rows, channels = features_ref.shape
    classes = head_ref.shape[0]
    north = rows // 8
    wide = rows + 16

    loads[0].wait()
    loads[1].wait()
    fill(features_ref, brick_ref, occupancy_ref, ext0_ref, own_ref)
    pl.semaphore_wait(barrier, len(devices))
    copies = exchange_start(own_ref, ext0_ref, send0, recv0)
    edge = jnp.zeros((size_e + 4, 16, 128), BF)
    own_ref[:, 0:16] = edge
    own_ref[:, 16 + rows : 32 + rows] = edge
    cols1[0 : 2 * wide] = jnp.zeros((2 * wide, cols1.shape[1]), BF)
    cols1[(size_e + 2) * wide :] = jnp.zeros((2 * wide, cols1.shape[1]), BF)
    build(own_ref, 2, size_e, 0, north + 2, cols1.at[2 * wide : (size_e + 2) * wide])
    loads[2].wait()
    lay_forward(w1_ref, wf1)
    convolve(cols1, wide, (size_e + 2) * wide, wf1, acc, True)
    loads[3].wait()
    lay_forward(w2_ref, wf2)
    wide_head[...] = jnp.zeros_like(wide_head)
    wide_head[0:classes, 0:channels] = head_ref[...]
    loads[4].wait()
    lay_teacher(teacher_ref, flat_teacher, turned)
    exchange_end(copies, ext0_ref)
    build_halo(ext0_ref, halo_cols)
    convolve_halo(halo_cols, wide, size_e, wf1, acc, True)

    def first(pair, carry):
        for half in range(2):
            i = pair * 2 + half
            at = pl.ds(pl.multiple_of(i * wide, 16), wide)
            x = ext0_ref[i + 1].astype(F32)[8 : 8 + wide]
            mask = jnp.broadcast_to(x[:, channels : channels + 1], (wide, 128))
            p1 = mask * acc[at]
            sig = jax.nn.sigmoid(p1)
            a1_ref[i] = (p1 * sig).astype(BF)
            slope_ref[at] = mask * slope_of(p1, sig)
        return carry

    lax.fori_loop(0, (size_e + 2) // 2, first, 0)
    build(a1_ref, 0, size_e + 2, 0, north, cols2)
    convolve(cols2, rows, size_e * rows, wf2, acc, True)
    head = wide_head[...]
    row = lax.broadcasted_iota(jnp.int32, (128, 128), 0)
    col = lax.broadcasted_iota(jnp.int32, (128, 128), 1)

    group = size_e

    def second(i, carry):
        planes = pl.ds(i * group + 2, group)
        at = pl.ds(pl.multiple_of(i * (group * rows), 128), group * rows)
        x = ext0_ref[planes, 16 : 16 + rows].astype(F32).reshape(group * rows, 128)
        mask = jnp.broadcast_to(x[:, channels : channels + 1], (group * rows, 128))
        p2 = mask * acc[at]
        sig = jax.nn.sigmoid(p2)
        a2 = (p2 * sig).astype(BF)
        logits = lax.dot_general(a2, head, NT, preferred_element_type=F32)
        teacher = []
        for b in range(group):
            pick = (row == col * size_e + (i * group + b)) & (col < classes)
            pick = jnp.where(pick, 1.0, 0.0).astype(BF)
            teacher.append(jnp.dot(turned[...], pick, preferred_element_type=F32))
        g = mask * (logits - jnp.concatenate(teacher, axis=0))
        high = g.astype(BF)
        left = g - high.astype(F32)
        mid = left.astype(BF)
        low = (left - mid.astype(F32)).astype(BF)
        back = jnp.dot(low, head, preferred_element_type=F32)
        back = back + jnp.dot(mid, head, preferred_element_type=F32)
        back = back + jnp.dot(high, head, preferred_element_type=F32)
        g2 = (mask * back * slope_of(p2, sig)).astype(BF)
        ext2_ref[planes, 16 : 16 + rows] = g2.reshape(group, rows, 128)
        gt_ref[:, at] = g2.astype(F32).T.astype(BF)
        return carry

    lax.fori_loop(0, size_e // group, second, 0)
    copies = exchange_start(ext2_ref, ext2_ref, send2, recv2)
    weight_grad(gt_ref, cols2, rows, part_ref)
    pack(part_ref, packed2_ref)
    next(two)
    lay_backward(w2_ref, wb2)
    build(ext0_ref, 1, size_e + 2, 1, north, cols0)
    next(two)
    exchange_end(copies, ext2_ref)
    build(ext2_ref, 0, size_e + 4, 0, north + 2, cols1)
    convolve(cols1, wide, (size_e + 2) * wide, wb2, acc, False)
    next(two)

    for i in range(size_e + 2):
        g1 = (acc[i * wide : (i + 1) * wide] * slope_ref[i * wide : (i + 1) * wide]).astype(BF)
        g1_ref[i] = g1
        if 0 < i <= size_e:
            gt_ref[:, (i - 1) * rows : i * rows] = g1.astype(F32)[8 : 8 + rows].T.astype(BF)
    weight_grad(gt_ref, cols0, rows, part_ref, 0, 2)
    pack(part_ref, packed1_ref, 0, 4)
    next(one_a)
    weight_grad(gt_ref, cols0, rows, part_ref, 2, 3)
    pack(part_ref, packed1_ref, 4, 6)
    next(one_b)
    next(one_a)
    next(one_b)
    lay_backward(w1_ref, wb1)
    build(g1_ref, 0, size_e + 2, 0, north, cols2)
    next(two)
    convolve(cols2, rows, size_e * rows, wb1, acc, False)

    def last(i, carry):
        at = pl.ds(pl.multiple_of(i * rows, 16), rows)
        x = ext0_ref[i + 2, 16 : 16 + rows].astype(F32)
        mask = jnp.broadcast_to(x[:, channels : channels + 1], (rows, 128))
        out_ref[i] = (mask * acc[at])[:, 0:channels].astype(BF)
        return carry

    lax.fori_loop(0, size_e, last, 0)
    saved = pltpu.make_async_copy(out_ref, out_hbm, local.at[0])
    saved.start()
    next(one_a)
    next(one_b)
    next(two)
    next(one_a)
    next(one_b)
    next(two)
    put2 = pltpu.make_async_copy(rest[0], full2_hbm, local.at[1])
    put2.start()
    next(one_a)
    next(one_b)
    next(one_a)
    put1a = pltpu.make_async_copy(rest[8], full1_hbm.at[0:split], local.at[2])
    put1a.start()
    next(one_b)
    put1b = pltpu.make_async_copy(rest[16], full1_hbm.at[pl.ds(split, split)], local.at[3])
    put1b.start()
    saved.wait()
    put2.wait()
    put1a.wait()
    put1b.wait()


def finish_kernel(
    scale, out_in, full1_in, full2_in, out_hbm, grad1_hbm, grad2_hbm,
    out_ref, full1_ref, full2_ref, grad1_ref, grad2_ref, loads, stores1, stores2,
):
    pairs = ((full2_in, full2_ref), (full1_in, full1_ref), (out_in, out_ref))
    copies = [pltpu.make_async_copy(a, b, loads.at[i]) for i, (a, b) in enumerate(pairs)]
    for copy in copies:
        copy.start()
    copies[0].wait()
    stores = unpack(full2_ref, grad2_ref, scale, grad2_hbm, stores2)
    copies[1].wait()
    stores += unpack(full1_ref, grad1_ref, scale, grad1_hbm, stores1)
    copies[2].wait()
    saved = pltpu.make_async_copy(out_ref, out_hbm, loads.at[3])
    saved.start()
    for copy in stores + [saved]:
        copy.wait()


def per_device(
    features, brick_active, voxel_occupancy, first_weights, second_weights, head, teacher
):
    channels, east, north, upward = features.shape
    classes = head.shape[0]
    rows = north * upward
    shape = jax.ShapeDtypeStruct
    sems = pltpu.SemaphoreType.DMA
    wide = rows + 16
    ext = VM((east + 4, rows + 32, 128), BF)
    field = VM((east + 2, wide, 128), BF)
    weights = VM(first_weights.shape, BF)
    forward, backward = VM((3, 128, 1152), BF), VM((3, 1152, 128), BF)
    narrow_cols = VM(((east + 2) * rows, 1152), BF)
    out = shape((east, rows, channels), BF)
    full = shape((PACKED, 128), BF)
    grad = shape((27, channels, channels), F32)
    vmem, anywhere = pl.BlockSpec(memory_space=VM), pl.BlockSpec(memory_space=pl.ANY)
    packed = VM((PACKED, 128), F32)
    result = pl.pallas_call(
        main_kernel,
        out_shape=(out, full, full),
        in_specs=[anywhere, pl.BlockSpec(memory_space=pltpu.SMEM), anywhere, anywhere, anywhere, vmem, anywhere],
        out_specs=[anywhere] * 3,
        scratch_shapes=[
            ext, ext, VM((4 * wide + 32 * east, 1152), BF), ext, weights, weights, forward, forward, backward, backward,
            VM((128, 128), BF),
            VM((classes * east * upward, north), F32),
            VM((128, 128), BF),
            narrow_cols, VM(((east + 4) * wide, 1152), BF), narrow_cols,
            VM(((east + 2) * wide, 128), F32),
            field,
            VM(((east + 2) * wide, 128), F32),
            field,
            VM((128, east * rows), BF),
            VM((27, channels, 128), F32),
            packed, packed,
            VM((east, rows, channels), BF),
            VM((east, rows, channels), BF),
            VM((east, upward, north), jnp.int32),
            VM(head.shape[:1] + (east, upward, north), BF),
            sems((8,)), sems((8,)), sems((8,)), sems((8,)), sems((8,)),
        ]
        + [
            item
            for size in (PACKED, PACKED // 2, PACKED // 2)
            for item in reduce_scratch(size, lax.axis_size("north") * 2, lax.axis_size("east") // 4)
        ],
        compiler_params=pltpu.CompilerParams(
            collective_id=1, has_side_effects=True, vmem_limit_bytes=60 << 20
        ),
    )(
        features.transpose(1, 2, 3, 0).reshape(east, rows, channels),
        brick_active.reshape(-1),
        voxel_occupancy.transpose(0, 2, 1),
        first_weights,
        second_weights,
        head,
        teacher.transpose(0, 1, 3, 2),
    )
    total_voxels = lax.axis_size("east") * lax.axis_size("north") * east * north * upward
    scale = 1.0 / math.sqrt(total_voxels)
    grad_features, grad_first, grad_second = pl.pallas_call(
        functools.partial(finish_kernel, scale),
        out_shape=(out, grad, grad),
        in_specs=[anywhere] * 3,
        out_specs=[anywhere] * 3,
        scratch_shapes=[VM(a.shape, a.dtype) for a in (out, full, full, grad, grad)]
        + [sems((4,)), sems((7,)), sems((7,))],
        compiler_params=pltpu.CompilerParams(vmem_limit_bytes=60 << 20),
    )(*result)
    grad_features = grad_features.reshape(east, north, upward, channels).transpose(3, 0, 1, 2)
    return (grad_features, grad_first, grad_second)


def solution(mesh):
    in_specs = (
        P(None, "east", "north", None),
        P("east", "north", None),
        P("east", "north", None),
        P(),
        P(),
        P(),
        P(None, "east", "north", None),
    )
    out_specs = (P(None, "east", "north", None), P(), P())
    return jax.shard_map(
        per_device, mesh=mesh, in_specs=in_specs, out_specs=out_specs, check_vma=False
    )
```
